32 devices in a mesh: groups: 2 (over y), space: 8 (over z, x), views: 2 (over core).
Axes of the slice: x: 2, y: 2, z: 4, core: 2. Of those that a mesh axis runs over, the one named last changes fastest.
Arguments:
- acquired_images: bfloat16 [8, 256, 8, 128], P('views', ('groups', 'space')), parts along dimension 1, may hold values from -6 to 6
- blur_profile_coefficients: float32 [8, 2, 3, 21], P('views'), may hold values from 0.01 to 0.1
- specimen_coverage: int32 [8, 16, 8], P('views', ('groups', 'space')), parts along dimension 1, may hold values from 0 to 1
- cleaned_estimate: float32 [256, 8, 128], P(('groups', 'space', 'views')), parts along dimension 0, may hold values from -16 to 16
- lagrange_multiplier: float32 [256, 8, 128], P(('groups', 'space', 'views')), parts along dimension 0, may hold values from -2 to 2
- lifting_kernel: float32 [48, 27], replicated, may hold values from -1.25 to 1.25
- standardize_factor: float32 [48], replicated, may hold values from 0.1 to 1.9
- triple_lifting_kernel: bfloat16 [144, 48], replicated, may hold values from -0.875 to 0.875
- per_channel_kernel: float32 [144, 27], replicated, may hold values from -1.25 to 1.25
- sharpness_factor: float32 [4], replicated, may hold values from 0.5 to 8
- mixing_back_kernel: bfloat16 [48, 48], replicated, may hold values from -0.875 to 0.875
- final_mapping_kernel: float32 [48], replicated, may hold values from -0.875 to 0.875
Outputs:
- new_denoised: float32 [256, 8, 128], P(('groups', 'space', 'views')), parts along dimension 0
- new_dual: float32 [256, 8, 128], P(('groups', 'space', 'views')), parts along dimension 0
The draws below stay inside these ranges and needn't reach their ends.
There are 2 independent parts, one for each index of `groups`. The reference program is written for one: setup_inputs(seed, part) draws one part's arguments, and reference() takes and returns one part's arrays. A program takes and returns all parts, laid end to end along the dimension named above; an argument that names none is the same for every part. Nothing has to cross between parts.
All inputs are finite; a program needn't handle non-finite values.
Results may differ from the reference program's by a relative error of at most 0.00035.
The reference program's roundings to bfloat16 on the way (of `normed`, `projected`, `mixed`, `weights` and `attended`) count: a program that leaves them out, or rounds other values in their place, can miss the bound.
Values may be sent and summed in bfloat16 or wider, within the bound.
A program may use at most 64 MiB of HBM per device.

```python
import math
import jax
import jax.numpy as jnp
from jax import lax

V = 8
BX = 16
NZ = 8
NY = 128
TILE = 16
TAPS = 21
RANK = 2
C = 48
MIXER_BRANCHES = 4
HD = 12
NX = 128
N_SPACE = 8


def draw_cleaned_estimate(key, part):
    keys = jax.random.split(key, 4)
    volume_shape = (NX, NZ, NY)
    row_pos = lax.broadcasted_iota(jnp.float32, volume_shape, 0) / NX
    plane_pos = lax.broadcasted_iota(jnp.float32, volume_shape, 1) / NZ
    col_pos = lax.broadcasted_iota(jnp.float32, volume_shape, 2) / NY
    ramp = 1.0 + 2.0 * row_pos
    tiles = 0.3 * jnp.exp(jax.random.uniform(keys[0], (NX // TILE, 1, NY // TILE), jnp.float32) * math.log(10.0))
    scale = jnp.repeat(jnp.repeat(tiles, TILE, axis=0), TILE, axis=2)
    freqs = jax.random.randint(keys[1], (3,), 1, 4).astype(jnp.float32)
    phase = jax.random.uniform(keys[2], (), jnp.float32, -math.pi, math.pi)
    wave = jnp.sin(2.0 * math.pi * (freqs[0] * row_pos + freqs[1] * plane_pos + freqs[2] * col_pos) + phase)
    noise = jnp.clip(jax.random.normal(keys[3], volume_shape, jnp.float32), -4.0, 4.0)
    smooth = 0.8 * wave
    return ramp * scale * 0.4 * noise + smooth


def draw_specimen_coverage(key, part):
    keys = jax.random.split(key, 5)
    tiles_x = NX // TILE
    tiles_y = NY // TILE
    centre_x = jax.random.randint(keys[0], (V, 1, 1), 0, tiles_x)
    centre_y = jax.random.randint(keys[1], (V, 1, 1), 0, tiles_y)
    reach_x = jax.random.randint(keys[2], (V, 1, 1), tiles_x // 4, tiles_x // 2 - 1)
    reach_y = jax.random.randint(keys[3], (V, 1, 1), max(tiles_y // 4, 1), tiles_y // 2 + 1)
    grid_x = lax.broadcasted_iota(jnp.int32, (V, tiles_x, tiles_y), 1) - centre_x
    grid_y = lax.broadcasted_iota(jnp.int32, (V, tiles_x, tiles_y), 2) - centre_y
    inside = grid_x * grid_x * reach_y * reach_y + grid_y * grid_y * reach_x * reach_x <= reach_x * reach_x * reach_y * reach_y
    holes = jax.random.randint(keys[4], (V, tiles_x, tiles_y), 0, 8) > 0
    centre_tile = (grid_x == 0) & (grid_y == 0)
    return (inside & (holes | centre_tile)).astype(jnp.int32)


def steps_of(rng, extent, cuts, least, high):
    level = 1.0
    for dim, parts in cuts:
        heights = jax.random.uniform(jax.random.fold_in(jax.random.fold_in(rng, 6), dim), (parts,), jnp.float32, least / len(cuts), high / len(cuts))
        level = level * jnp.repeat(jnp.exp(heights), extent[dim] // parts).reshape((-1,) + (1,) * (len(extent) - 1 - dim))
    return level


def scatter_about(stream_key, shape, width, reach, pieces=(), held_as=jnp.bfloat16):
    array = width * jax.random.normal(stream_key, shape, jnp.float32)
    if pieces:
        array = array * steps_of(stream_key, shape, pieces, -0.22, 0.18)
    return jnp.clip(array, -reach, reach).astype(held_as)


def setup_inputs(seed: int = 0, part: int = 0) -> dict:
    seeds = jax.random.split(jax.random.key(seed), 13)
    part_splits = jax.random.split(jax.random.fold_in(seeds[12], part), 13)
    return {
        "acquired_images": scatter_about(part_splits[0], (V, NX, NZ, NY), 1.0, 6.0, ((0, 2), (1, 8))),
        "blur_profile_coefficients": jnp.clip(jnp.exp(math.log(0.1) - 2.3025851 * jax.random.uniform(seeds[1], (V, RANK, 3, TAPS), jnp.float32) ** steps_of(seeds[1], (V, RANK, 3, TAPS), ((0, 2),), -0.2, 0.2)), 0.01, 0.1),
        "specimen_coverage": draw_specimen_coverage(jax.random.fold_in(jax.random.fold_in(seeds[12], part), 71), part),
        "cleaned_estimate": draw_cleaned_estimate(jax.random.fold_in(jax.random.fold_in(seeds[12], part), 71), part),
        "lagrange_multiplier": scatter_about(part_splits[4], (NX, NZ, NY), 0.3, 2.0, ((0, 16),), jnp.float32),
        "lifting_kernel": scatter_about(seeds[5], (C, 27), 27 ** -0.5, 1.25, (), jnp.float32),
        "standardize_factor": jnp.clip(1.0 + 0.18 * jax.random.normal(seeds[6], (C,), jnp.float32), 0.1, 1.9),
        "triple_lifting_kernel": scatter_about(seeds[7], (3 * C, C), C ** -0.5, 0.875),
        "per_channel_kernel": scatter_about(seeds[8], (3 * C, 27), 27 ** -0.5, 1.25, (), jnp.float32),
        "sharpness_factor": jnp.clip(jnp.exp(jax.random.uniform(seeds[9], (MIXER_BRANCHES,), jnp.float32, math.log(0.5), math.log(8.0))), 0.5, 8.0),
        "mixing_back_kernel": scatter_about(seeds[10], (C, C), C ** -0.5, 0.875),
        "final_mapping_kernel": scatter_about(seeds[11], (C,), C ** -0.5, 0.875, (), jnp.float32),
    }


highest = lax.Precision.HIGHEST
step_size = 0.5

def band_matrix(tap_values, out_count, in_count, direction, offset):
    out_rows = lax.broadcasted_iota(jnp.int32, (out_count, in_count), 0)
    in_cols = lax.broadcasted_iota(jnp.int32, (out_count, in_count), 1)
    distance = direction * (in_cols - out_rows) + offset
    total = jnp.zeros((out_count, in_count), tap_values.dtype)
    for tap_index in range(tap_values.shape[0]):
        total = total + jnp.where(distance == tap_index, tap_values[tap_index], jnp.zeros((), tap_values.dtype))
    return total

def tile_cells(field, tiles):
    row_count, plane_count, col_count = field.shape
    shaped = field.reshape(tiles.shape[0], row_count // tiles.shape[0], plane_count, tiles.shape[1], col_count // tiles.shape[1])
    masked = shaped * tiles.astype(field.dtype)[:, None, None, :, None]
    return masked.reshape(row_count, plane_count, col_count)

def shift_sum(field, tap_values, mirrored):
    half_taps = (tap_values.shape[0] - 1) // 2
    row_count = field.shape[0]
    padded = jnp.pad(field, ((half_taps, half_taps), (0, 0), (0, 0)))
    total = jnp.zeros_like(field)
    for tap_index in range(tap_values.shape[0]):
        begin = 2 * half_taps - tap_index if mirrored else tap_index
        total = total + tap_values[tap_index] * padded[begin:begin + row_count]
    return total

def lateral_matrices(view_taps, rank_index, plane_count, col_count):
    half_taps = (view_taps.shape[2] - 1) // 2
    along_y = band_matrix(view_taps[rank_index, 1], col_count, col_count, 1, half_taps)
    along_z = band_matrix(view_taps[rank_index, 2], plane_count, plane_count, 1, half_taps)
    return (along_y, along_z)

def blur_forward(field, view_taps):
    total = jnp.zeros_like(field)
    for rank_index in range(view_taps.shape[0]):
        along_y, along_z = lateral_matrices(view_taps, rank_index, field.shape[1], field.shape[2])
        blurred = shift_sum(field, view_taps[rank_index, 0], False)
        blurred = jnp.einsum('xzy,wy->xzw', blurred, along_y, precision=highest)
        blurred = jnp.einsum('xzy,wz->xwy', blurred, along_z, precision=highest)
        total = total + blurred
    return total

def blur_adjoint(field, view_taps):
    total = jnp.zeros_like(field)
    for rank_index in range(view_taps.shape[0]):
        along_y, along_z = lateral_matrices(view_taps, rank_index, field.shape[1], field.shape[2])
        spread = jnp.einsum('xwy,wz->xzy', field, along_z, precision=highest)
        spread = jnp.einsum('xzw,wy->xzy', spread, along_y, precision=highest)
        total = total + shift_sum(spread, view_taps[rank_index, 0], True)
    return total

def embed_rows(rows_in, lifting_kernel):
    count = rows_in.shape[0] - 2
    plane_count, col_count = (rows_in.shape[1], rows_in.shape[2])
    framed = jnp.pad(rows_in, ((0, 0), (1, 1), (1, 1)))
    windows = jnp.stack([framed[row_step:row_step + count, plane_step:plane_step + plane_count, col_step:col_step + col_count] for row_step in range(3) for plane_step in range(3) for col_step in range(3)])
    return jnp.einsum('ct,txzy->cxzy', lifting_kernel, windows, precision=highest)

def channel_norm(features, standardize_factor):
    centre = lax.optimization_barrier(jnp.mean(features, axis=0))
    deviation = features - centre
    spread = lax.optimization_barrier(jnp.mean(deviation * deviation, axis=0))
    return (deviation * lax.rsqrt(spread + 1e-05) * standardize_factor[:, None, None, None]).astype(jnp.bfloat16)

def depthwise(extended, per_channel_kernel):
    count = extended.shape[1] - 2
    plane_count, col_count = (extended.shape[2], extended.shape[3])
    framed = jnp.pad(extended, ((0, 0), (0, 0), (1, 1), (1, 1)))
    total = jnp.zeros((extended.shape[0], count, plane_count, col_count), jnp.float32)
    tap_index = 0
    for row_step in range(3):
        for plane_step in range(3):
            for col_step in range(3):
                window = framed[:, row_step:row_step + count, plane_step:plane_step + plane_count, col_step:col_step + col_count]
                total = total + per_channel_kernel[:, tap_index][:, None, None, None] * window.astype(jnp.float32)
                tap_index = tap_index + 1
    return total.astype(jnp.bfloat16)

def reference(acquired_images, blur_profile_coefficients, specimen_coverage, cleaned_estimate, lagrange_multiplier, lifting_kernel, standardize_factor, triple_lifting_kernel, per_channel_kernel, sharpness_factor, mixing_back_kernel, final_mapping_kernel):
    start_field = cleaned_estimate - lagrange_multiplier
    gradient = jnp.zeros_like(start_field)
    for view_index in range(V):
        evolved = blur_forward(start_field, blur_profile_coefficients[view_index])
        residual = tile_cells(evolved - acquired_images[view_index].astype(jnp.float32), specimen_coverage[view_index])
        gradient = gradient + blur_adjoint(residual, blur_profile_coefficients[view_index])
    fine = start_field - step_size * gradient
    padded = jnp.pad(fine, ((2, 2), (0, 0), (0, 0)))
    starts = jnp.arange(N_SPACE, dtype=jnp.int32) * BX

    def block_fields(start):
        rows_in = lax.dynamic_slice_in_dim(padded, start, BX + 4, 0)
        features = embed_rows(rows_in, lifting_kernel)
        normed = channel_norm(features, standardize_factor)
        projected = jnp.dot(triple_lifting_kernel, normed.reshape(C, -1), preferred_element_type=jnp.float32)
        projected = projected.reshape(3 * C, BX + 2, NZ, NY).astype(jnp.bfloat16)
        row_ids = start - 1 + jnp.arange(BX + 2, dtype=jnp.int32)
        inside = (row_ids >= 0) & (row_ids < NX)
        projected = jnp.where(inside[None, :, None, None], projected, jnp.zeros((), projected.dtype))
        return (features[:, 1:-1], depthwise(projected, per_channel_kernel))

    def block_stats(start):
        unused, mixed = block_fields(start)
        queries = mixed[:C].astype(jnp.float32)
        keys_part = mixed[C:2 * C].astype(jnp.float32)
        inner_products = jnp.einsum('hin,hjn->hij', queries.reshape(MIXER_BRANCHES, HD, -1), keys_part.reshape(MIXER_BRANCHES, HD, -1))
        return (inner_products, lax.optimization_barrier(jnp.sum(queries * queries, axis=(1, 2, 3))), lax.optimization_barrier(jnp.sum(keys_part * keys_part, axis=(1, 2, 3))))
    grams, squares_q, squares_k = lax.map(block_stats, starts)
    inner_products = lax.optimization_barrier(jnp.sum(grams, axis=0))
    request_lengths = jnp.sqrt(lax.optimization_barrier(jnp.sum(squares_q, axis=0)) + 1e-06).reshape(MIXER_BRANCHES, HD)
    lookup_lengths = jnp.sqrt(lax.optimization_barrier(jnp.sum(squares_k, axis=0)) + 1e-06).reshape(MIXER_BRANCHES, HD)
    affinity_logits = sharpness_factor[:, None, None] * inner_products / (request_lengths[:, :, None] * lookup_lengths[:, None, :])
    raised = jnp.exp(affinity_logits)
    weights = (raised / lax.optimization_barrier(jnp.sum(raised, axis=2, keepdims=True))).astype(jnp.bfloat16)

    def block_output(start):
        features, mixed = block_fields(start)
        values = mixed[2 * C:].astype(jnp.float32).reshape(MIXER_BRANCHES, HD, -1)
        attended = jnp.einsum('hij,hjn->hin', weights.astype(jnp.float32), values).astype(jnp.bfloat16)
        projected = jnp.dot(mixing_back_kernel, attended.reshape(C, -1), preferred_element_type=jnp.float32)
        combined = features + projected.reshape(features.shape)
        update = jnp.einsum('c,cxzy->xzy', final_mapping_kernel, combined, precision=highest)
        fine_rows = lax.dynamic_slice_in_dim(fine, start, BX, 0)
        dual_rows = lax.dynamic_slice_in_dim(lagrange_multiplier, start, BX, 0)
        new_rows = fine_rows + update
        return (new_rows, dual_rows + fine_rows - new_rows)
    new_blocks, dual_blocks = lax.map(block_output, starts)
    return (new_blocks.reshape(NX, NZ, NY), dual_blocks.reshape(NX, NZ, NY))
```

```python
import functools

import jax
import jax.numpy as jnp
from jax import lax
from jax.experimental import pallas as pl
from jax.experimental.pallas import tpu as pltpu
from jax.sharding import PartitionSpec as P

highest = lax.Precision.HIGHEST
step_size = 0.5
MESH = pl.DeviceIdType.MESH
f32 = jnp.float32
bf16 = jnp.bfloat16
RELATIONS = ((0, 1), (-1, 0), (-1, 1), (1, 0), (1, 1))


def halves(value):
    high = value.astype(bf16)
    low = (value - high.astype(f32)).astype(bf16)
    return high, low


def dot3(left, right):
    lh, ll = left
    rh, rl = right
    return (
        jnp.dot(lh, rh, preferred_element_type=f32)
        + jnp.dot(lh, rl, preferred_element_type=f32)
        + jnp.dot(ll, rh, preferred_element_type=f32)
    )


NT = (((1,), (1,)), ((), ()))
TN = (((0,), (0,)), ((), ()))


def dotg3(left, right, dims):
    lh, ll = left
    rh, rl = right
    total = None
    for first, second in ((lh, rh), (lh, rl), (ll, rh)):
        term = lax.dot_general(first, second, dims, preferred_element_type=f32)
        total = term if total is None else total + term
    return total


def thirds(value):
    high = value.astype(bf16)
    rest = value - high.astype(f32)
    middle = rest.astype(bf16)
    low = (rest - middle.astype(f32)).astype(bf16)
    return high, middle, low


def iota(shape, dim):
    return lax.broadcasted_iota(jnp.int32, shape, dim)


def row_of(scalars, count):
    lane = iota((1, 128), 1)
    row = jnp.zeros((1, 128), f32)
    for c in range(count):
        row = jnp.where(lane == c, scalars[c], row)
    return row[:, 0:count]


def kernel(
    space, taps_hbm, cover_hbm, final_hbm, gain_hbm, sharp_hbm, lift_hbm, weights_hbm,
    channel_hbm, back_hbm, images_hbm, cleaned_hbm, lagrange_hbm, update_out, fine_out,
    taps, cover, final_in, gain_in, sharp_in, tap_rows, lift_in, weights_in, taps_in,
    back_in, images, cleaned, lagrange, field, wide, part, parts_in, rows_pad,
    y_high, y_low, z_high, z_low, lift, lift_final, weights, channel_taps,
    stack, deviations, bands, conv, mixed, stats, gathered,
    local, send1, recv1, send2, recv2, send3, recv3,
):
    group = lax.axis_index("groups")
    s = lax.axis_index("space")
    w = lax.axis_index("views")
    me = 2 * s + w
    count = 2 * space

    loads = [
        pltpu.make_async_copy(cleaned_hbm, cleaned, local.at[0]),
        pltpu.make_async_copy(lagrange_hbm, lagrange, local.at[1]),
        pltpu.make_async_copy(taps_hbm, taps, local.at[2]),
        pltpu.make_async_copy(taps_hbm, tap_rows, local.at[3]),
        pltpu.make_async_copy(images_hbm, images, local.at[4]),
        pltpu.make_async_copy(cover_hbm, cover, local.at[5]),
        pltpu.make_async_copy(final_hbm, final_in, local.at[6]),
        pltpu.make_async_copy(gain_hbm, gain_in, local.at[7]),
        pltpu.make_async_copy(sharp_hbm, sharp_in, local.at[8]),
        pltpu.make_async_copy(lift_hbm, lift_in, local.at[9]),
        pltpu.make_async_copy(weights_hbm, weights_in, local.at[10]),
        pltpu.make_async_copy(channel_hbm, taps_in, local.at[11]),
        pltpu.make_async_copy(back_hbm, back_in, local.at[12]),
    ]
    for load in loads:
        load.start()

    def present(ds):
        if ds < 0:
            return s > 0
        if ds > 0:
            return s < space - 1
        return s >= 0

    def other(flip):
        return 1 - w if flip else w

    def peer(step):
        return lax.rem(me + step, count)

    barrier = pltpu.get_barrier_semaphore()

    def greet(step, carry):
        to = peer(step)
        pl.semaphore_signal(
            barrier, inc=1, device_id=(group, to // 2, lax.rem(to, 2)), device_id_type=MESH
        )
        return carry

    lax.fori_loop(1, count, greet, 0)

    loads[0].wait()
    loads[1].wait()
    field[...] = cleaned[...] - lagrange[...]
    wide[pl.ds(16 + 8 * w, 8)] = field[...]

    @pl.when(s == 0)
    def _():
        wide[0:16] = jnp.zeros((16,) + wide.shape[1:], f32)

    @pl.when(s == space - 1)
    def _():
        wide[32:48] = jnp.zeros((16,) + wide.shape[1:], f32)

    pl.semaphore_wait(barrier, count - 1)

    def first(k, ds, flip, sender_w):
        begin, size = 0, 8
        if (ds, sender_w) == (1, 0):
            begin, size = 6, 2
        if (ds, sender_w) == (-1, 1):
            begin, size = 0, 2
        return pltpu.make_async_remote_copy(
            src_ref=field.at[pl.ds(begin, size)],
            dst_ref=wide.at[pl.ds(16 * (1 - ds) + 8 * sender_w + begin, size)],
            send_sem=send1.at[k],
            recv_sem=recv1.at[k],
            device_id=(group, s + ds, other(flip)),
            device_id_type=MESH,
        )

    for k, (ds, flip) in enumerate(RELATIONS):
        for core in range(2):

            @pl.when(present(ds) & (w == core))
            def _():
                first(k, ds, flip, core).start()

    for load in loads[2:]:
        load.wait()
    part[...] = jnp.zeros_like(part)
    rows = iota((128, 128), 0)
    cols = iota((128, 128), 1)
    keep_y = jnp.abs(rows - cols) <= 10
    keep_z = (rows // 8) == (cols // 8)
    lane_tile = iota((8, 128), 1) // 16
    rows_pad[...] = jnp.zeros_like(rows_pad)
    rows_pad[:, :, :, 0:21] = tap_rows[...]

    def build(v, carry):
        for r in range(2):
            for dim, keep, high_ref, low_ref in (
                (1, keep_y, y_high, y_low),
                (2, keep_z, z_high, z_low),
            ):
                row = pltpu.roll(rows_pad[v, dim], 118, 1)[r : r + 1]
                spread = pltpu.roll(
                    jnp.broadcast_to(row, (128, 128)), 0, 1, stride=1, stride_axis=0
                )
                high, low = halves(jnp.where(keep, spread, 0.0))
                high_ref[2 * v + r] = high
                low_ref[2 * v + r] = low
        return carry

    lax.fori_loop(0, images.shape[0], build, 0)

    final_row = row_of(final_in, 48)
    gain_row = row_of(gain_in, 48)
    row48 = iota((48, 48), 0)
    col48 = iota((48, 48), 1)
    gain = jnp.sum(jnp.where(row48 == col48, gain_row, 0.0), axis=1, keepdims=True)
    gain_wide = jnp.broadcast_to(gain, (48, 1280))
    kernel_t = lift_in[...]
    centred = thirds(kernel_t - jnp.sum(kernel_t, axis=1, keepdims=True) * (1.0 / 48.0))
    mapped = thirds(
        jnp.broadcast_to(jnp.sum(kernel_t * final_row, axis=1, keepdims=True), (27, 16))
    )
    spot = iota((27, 512), 1)
    segment = spot // 80
    inner = lax.rem(spot, 80)
    sub = lax.rem(inner, 8)
    start_tap = 9 * (lax.rem(inner, 24) // 8) + inner // 24
    row16 = iota((16, 512), 0)
    lift_final[...] = jnp.zeros_like(lift_final)

    def build_lift(z, carry):
        step = sub - z + 1
        fits = (step >= 0) & (step <= 2) & (inner < 72)
        fits = fits & (iota((27, 512), 0) == start_tap + 3 * step)
        tables = (
            jnp.where(fits & ((segment <= 1) | (segment == 4)), 1.0, 0.0).astype(bf16),
            jnp.where(fits & ((segment == 2) | (segment == 3)), 1.0, 0.0).astype(bf16),
            jnp.where(fits & (segment == 5), 1.0, 0.0).astype(bf16),
        )

        def expand(pieces):
            total = None
            for piece, table in zip(pieces, tables):
                term = lax.dot_general(piece, table, TN, preferred_element_type=f32)
                total = term if total is None else total + term
            return total.astype(bf16)

        lift[z] = expand(centred)
        here = jnp.where(row16 == z, expand(mapped).astype(f32), 0.0)
        lift_final[...] = (lift_final[...].astype(f32) + here).astype(bf16)
        return carry

    lax.fori_loop(0, 8, build_lift, 0)
    eye48 = jnp.where(row48 == col48, 1.0, 0.0)
    weights[...] = lax.dot_general(
        weights_in[...], eye48.astype(bf16), TN, preferred_element_type=f32
    ).astype(bf16)
    eye27 = jnp.where(iota((27, 128), 0) == iota((27, 128), 1), 1.0, 0.0)
    channel_taps[...] = lax.dot_general(
        taps_in[...], eye27, TN, precision=highest, preferred_element_type=f32
    )
    back = jnp.dot(
        final_row, back_in[...].astype(f32), precision=highest, preferred_element_type=f32
    )

    for k, (ds, flip) in enumerate(RELATIONS):
        for core in range(2):

            @pl.when(present(ds) & (w == core))
            def _():
                first(k, ds, flip, core).wait_send()

            @pl.when(present(-ds) & (other(flip) == core))
            def _():
                first(k, ds, flip, core).wait_recv()

    def view_step(v, carry):
        total = jnp.zeros((128, 128), f32)
        for r in range(2):
            acc = taps[v, 0, r, 0] * wide[6:22]
            for a in range(1, 21):
                acc = acc + taps[v, 0, r, a] * wide[6 + a : 22 + a]
            along_y = y_high[2 * v + r], y_low[2 * v + r]
            along_z = z_high[2 * v + r], z_low[2 * v + r]
            moved = dotg3(halves(acc.reshape(128, 128)), along_y, NT)
            total = total + dot3(along_z, halves(moved))
        mask = jnp.zeros((8, 128), f32)
        for j in range(8):
            mask = jnp.where(lane_tile == j, cover[v, 0, j].astype(f32), mask)
        residual = (total.reshape(16, 8, 128) - images[v].astype(f32)) * mask[None]
        parted = halves(residual.reshape(128, 128))
        out = [None] * 36
        for r in range(2):
            along_y = y_high[2 * v + r], y_low[2 * v + r]
            along_z = z_high[2 * v + r], z_low[2 * v + r]
            spread = dot3(halves(dotg3(along_z, parted, TN)), along_y).reshape(16, 8, 128)
            for q in range(16):
                row = spread[q]
                for a in range(21):
                    term = taps[v, 0, r, a] * row
                    out[q + a] = term if out[q + a] is None else out[q + a] + term
        for p in range(36):
            part[8 + p] = part[8 + p] + out[p]
        return carry

    lax.fori_loop(0, images.shape[0], view_step, 0)

    def second(k, ds, flip, target):
        begin, size = 0, 12
        if (ds, target) == (-1, 0):
            begin, size = 8, 4
        if (ds, target) == (1, 1):
            begin, size = 0, 4
        return pltpu.make_async_remote_copy(
            src_ref=part.at[pl.ds(8 * target + 16 + 16 * ds + begin, size)],
            dst_ref=parts_in.at[k, pl.ds(begin, size)],
            send_sem=send2.at[k],
            recv_sem=recv2.at[k],
            device_id=(group, s + ds, target),
            device_id_type=MESH,
        )

    for k, (ds, flip) in enumerate(RELATIONS):
        for core in range(2):

            @pl.when(present(ds) & (other(flip) == core))
            def _():
                second(k, ds, flip, core).start()

        @pl.when(jnp.logical_not(present(-ds)))
        def _():
            parts_in[k] = jnp.zeros(parts_in.shape[1:], f32)

        if ds == -1:

            @pl.when(present(1) & (w == 0))
            def _():
                parts_in[k, 0:8] = jnp.zeros((8,) + parts_in.shape[2:], f32)

        if ds == 1:

            @pl.when(present(-1) & (w == 1))
            def _():
                parts_in[k, 4:12] = jnp.zeros((8,) + parts_in.shape[2:], f32)

    split_taps = jnp.concatenate(halves(channel_taps[...][:, 0:27]), axis=0)
    spot_c = iota((27, 576), 1)
    shift = spot_c // 64
    plane_in = lax.rem(spot_c, 64) // 8
    tap_of = 9 * lax.rem(shift, 3) + shift // 3
    own = lax.rem(iota((8, 576), 1), 8) == iota((8, 576), 0)

    def build_conv(zz, carry):
        tiles = []
        for half in range(2):
            step = plane_in - (2 * zz + half) + 1
            fits = (step >= 0) & (step <= 2) & (iota((27, 576), 0) == tap_of + 3 * step)
            tiles.append(
                jnp.dot(
                    split_taps, jnp.where(fits, 1.0, 0.0).astype(bf16), preferred_element_type=f32
                )
            )
        at = pl.multiple_of(16 * zz, 16)
        for g in range(18):
            for part_of in range(2):
                row = 144 * part_of + 8 * g
                pair = [jnp.where(own, tile[row : row + 8], 0.0) for tile in tiles]
                conv[g, pl.ds(64 * part_of + at, 16), :] = jnp.concatenate(pair, axis=0).astype(
                    bf16
                )
        return carry

    lax.fori_loop(0, 4, build_conv, 0)

    for k, (ds, flip) in enumerate(RELATIONS):
        for core in range(2):

            @pl.when(present(ds) & (other(flip) == core))
            def _():
                second(k, ds, flip, core).wait_send()

            @pl.when(present(-ds) & (w == core))
            def _():
                second(k, ds, flip, core).wait_recv()

    gradient = part[pl.ds(8 * w + 16, 12)]
    for k in range(5):
        gradient = gradient + parts_in[k]
    fine = wide[pl.ds(14 + 8 * w, 12)] - step_size * gradient
    row_id = 16 * s + 8 * w - 2 + iota(fine.shape, 0)
    fine = jnp.where((row_id >= 0) & (row_id < 16 * space), fine, 0.0)
    fine_out[...] = fine[2:10]

    lane3 = iota(fine.shape, 2)
    before = jnp.where(lane3 == 0, 0.0, pltpu.roll(fine, 1, 2))
    after = jnp.where(lane3 == 127, 0.0, pltpu.roll(fine, 127, 2))
    for x in range(10):
        pieces = []
        for moved in (before, fine, after):
            pieces.append(moved[x : x + 3].reshape(24, 128))
        pieces.append(jnp.zeros((8, 128), f32))
        high, middle, low = thirds(jnp.concatenate(pieces, axis=0))
        at = slice(x * 128, (x + 1) * 128)
        for k, piece in enumerate((high, middle, high, middle, low, high)):
            stack[80 * k : 80 * k + 80, at] = piece
    stack[480:512] = jnp.zeros((32, 1280), bf16)
    update = jnp.dot(lift_final[...], stack[...], preferred_element_type=f32)

    wide_row = 16 * s + 8 * w - 1 + iota((48, 1280), 1) // 128
    inside = (wide_row >= 0) & (wide_row < 16 * space)

    deviations[...] = jnp.dot(
        lift[...].reshape(384, 512), stack[...], preferred_element_type=f32
    ).reshape(8, 48, 1280)

    lane16 = iota((16, 128), 1)

    def plane_pair(zz, carry):
        pair = []
        for half in range(2):
            dev = deviations[2 * zz + half]
            spread = jnp.sum(dev * dev, axis=0, keepdims=True) * (1.0 / 48.0)
            value = jnp.where(inside, dev * lax.rsqrt(spread + 1e-05) * gain_wide, 0.0)
            pair.append(jnp.dot(weights[...], value.astype(bf16), preferred_element_type=f32))
        rows = pl.ds(pl.multiple_of(16 * zz, 16), 16)
        for g in range(18):
            for x in range(10):
                at = slice(x * 128, (x + 1) * 128)
                cell = jnp.concatenate([proj[8 * g : 8 * g + 8, at] for proj in pair], axis=0)
                bands[0, g, rows, at] = jnp.where(lane16 == 0, 0.0, pltpu.roll(cell, 1, 1)).astype(
                    bf16
                )
                bands[1, g, rows, at] = cell.astype(bf16)
                bands[2, g, rows, at] = jnp.where(
                    lane16 == 127, 0.0, pltpu.roll(cell, 127, 1)
                ).astype(bf16)
        return carry

    lax.fori_loop(0, 4, plane_pair, 0)

    def channel_group(g, carry):
        at = pl.multiple_of(g * 8, 8)
        for n in range(4):
            pieces = []
            for dy in range(3):
                for dx in range(3):
                    begin = dx * 128 + n * 256
                    pieces.append(bands[dy, g, :, begin : begin + 256])
            both = jnp.dot(
                conv[g], jnp.concatenate(pieces, axis=0), preferred_element_type=f32
            )
            total = both[0:64] + both[64:128]
            for z in range(8):
                mixed[z, pl.ds(at, 8), n * 256 : (n + 1) * 256] = total[8 * z : 8 * z + 8]
        return carry

    lax.fori_loop(0, 12, channel_group, 0)

    def gram_step(z, total):
        value = mixed[z, 0:96].astype(bf16)
        return total + lax.dot_general(value, value, NT, preferred_element_type=f32)

    gram = lax.fori_loop(0, 8, gram_step, jnp.zeros((96, 96), f32), unroll=True)

    same = row48 // 12 == col48 // 12
    block = jnp.where(same, 1.0, 0.0)
    row16 = iota((16, 48), 0)
    col16 = iota((16, 48), 1)
    pick = jnp.where(lax.rem(col16, 12) == row16, 1.0, 0.0)
    kq = jnp.where(same, gram[48:96, 0:48], 0.0)
    squares_q = jnp.sum(jnp.where(row48 == col48, gram[0:48, 0:48], 0.0), axis=0, keepdims=True)
    squares_k = jnp.sum(jnp.where(row48 == col48, gram[48:96, 48:96], 0.0), axis=0, keepdims=True)
    packed = jnp.dot(pick, kq, precision=highest, preferred_element_type=f32)
    packed = jnp.where(row16 == 12, squares_q, packed)
    packed = jnp.where(row16 == 13, squares_k, packed)
    stats[...] = jnp.zeros_like(stats)
    stats[:, 0:48] = packed

    def share(step):
        to = peer(step)
        return pltpu.make_async_remote_copy(
            src_ref=stats,
            dst_ref=gathered.at[step],
            send_sem=send3.at[step],
            recv_sem=recv3.at[step],
            device_id=(group, to // 2, lax.rem(to, 2)),
            device_id_type=MESH,
        )

    def start(step, carry):
        share(step).start()
        return carry

    def finish(step, carry):
        share(step).wait()
        return carry

    lax.fori_loop(1, count, start, 0)
    gathered[0] = stats[...]
    lax.fori_loop(12, 18, channel_group, 0)
    lax.fori_loop(1, count, finish, 0)

    def add(step, total):
        slot = lax.rem(me - step + count, count)
        return total + gathered[slot][:, 0:48]

    summed = lax.fori_loop(0, count, add, jnp.zeros((16, 48), f32))
    squares_q = summed[12:13]
    squares_k = summed[13:14]
    lengths_k = jnp.dot(
        pick * jnp.sqrt(squares_k + 1e-06), block, precision=highest, preferred_element_type=f32
    )
    valid = row16 < 12
    head = iota((1, 48), 1) // 12
    sharp_row = jnp.zeros((1, 48), f32)
    for h in range(4):
        sharp_row = jnp.where(head == h, sharp_in[h], sharp_row)
    logits = sharp_row * summed / (jnp.sqrt(squares_q + 1e-06) * jnp.where(valid, lengths_k, 1.0))
    raised = jnp.where(valid, jnp.exp(jnp.where(valid, logits, 0.0)), 0.0)
    shares = (raised / jnp.sum(raised, axis=0, keepdims=True)).astype(bf16).astype(f32)
    placed_shares = lax.dot_general(
        shares, pick, TN, precision=highest, preferred_element_type=f32
    )
    placed_shares = jnp.where(same, placed_shares, 0.0).astype(bf16)
    back_high, back_low = halves(back)

    def value_plane(z, total):
        attended = jnp.dot(
            placed_shares, mixed[z, 96:144].astype(bf16), preferred_element_type=f32
        )
        back_rows = jnp.where(row16 == z, back_high.astype(f32), 0.0)
        back_rows = jnp.where(row16 == z + 8, back_low.astype(f32), back_rows)
        return total + jnp.dot(
            back_rows.astype(bf16), attended.astype(bf16), preferred_element_type=f32
        )

    added = lax.fori_loop(0, 8, value_plane, jnp.zeros((16, 1024), f32), unroll=True)
    extra = added[0:8] + added[8:16]
    for x in range(8):
        update_out[x] = (
            update[0:8, (x + 1) * 128 : (x + 2) * 128] + extra[:, x * 128 : (x + 1) * 128]
        )


def body(
    space,
    acquired_images,
    blur_profile_coefficients,
    specimen_coverage,
    cleaned_estimate,
    lagrange_multiplier,
    lifting_kernel,
    standardize_factor,
    triple_lifting_kernel,
    per_channel_kernel,
    sharpness_factor,
    mixing_back_kernel,
    final_mapping_kernel,
):
    vmem = pl.BlockSpec(memory_space=pltpu.VMEM)
    hbm = pl.BlockSpec(memory_space=pltpu.HBM)
    profiles = blur_profile_coefficients.transpose(0, 2, 1, 3)
    count = 2 * space
    shape = jax.ShapeDtypeStruct((8, 8, 128), f32)
    dma = pltpu.SemaphoreType.DMA
    update, fine = pl.pallas_call(
        functools.partial(kernel, space),
        out_shape=(shape, shape),
        in_specs=[hbm] * 12,
        out_specs=(vmem, vmem),
        scratch_shapes=[
            pltpu.SMEM((4, 3, 2, 21), f32),
            pltpu.SMEM((4, 1, 8), jnp.int32),
            pltpu.SMEM((48,), f32),
            pltpu.SMEM((48,), f32),
            pltpu.SMEM((4,), f32),
            pltpu.VMEM((4, 3, 2, 21), f32),
            pltpu.VMEM((27, 48), f32),
            pltpu.VMEM((48, 144), bf16),
            pltpu.VMEM((27, 144), f32),
            pltpu.VMEM((48, 48), bf16),
            pltpu.VMEM((4, 16, 8, 128), bf16),
            pltpu.VMEM((8, 8, 128), f32),
            pltpu.VMEM((8, 8, 128), f32),
            pltpu.VMEM((8, 8, 128), f32),
            pltpu.VMEM((48, 8, 128), f32),
            pltpu.VMEM((52, 8, 128), f32),
            pltpu.VMEM((5, 12, 8, 128), f32),
            pltpu.VMEM((4, 3, 2, 128), f32),
            pltpu.VMEM((8, 128, 128), bf16),
            pltpu.VMEM((8, 128, 128), bf16),
            pltpu.VMEM((8, 128, 128), bf16),
            pltpu.VMEM((8, 128, 128), bf16),
            pltpu.VMEM((8, 48, 512), bf16),
            pltpu.VMEM((16, 512), bf16),
            pltpu.VMEM((144, 48), bf16),
            pltpu.VMEM((144, 128), f32),
            pltpu.VMEM((512, 1280), bf16),
            pltpu.VMEM((8, 48, 1280), f32),
            pltpu.VMEM((3, 18, 64, 1280), bf16),
            pltpu.VMEM((18, 128, 576), bf16),
            pltpu.VMEM((8, 144, 1024), f32),
            pltpu.VMEM((16, 128), f32),
            pltpu.VMEM((count, 16, 128), f32),
            dma((13,)),
            dma((5,)),
            dma((5,)),
            dma((5,)),
            dma((5,)),
            dma((count,)),
            dma((count,)),
        ],
        compiler_params=pltpu.CompilerParams(
            collective_id=0, has_side_effects=True, vmem_limit_bytes=64 * 1024 * 1024
        ),
        name="iteration",
    )(
        profiles,
        specimen_coverage,
        final_mapping_kernel,
        standardize_factor,
        sharpness_factor,
        lifting_kernel.T,
        triple_lifting_kernel.T,
        per_channel_kernel.T,
        mixing_back_kernel,
        acquired_images,
        cleaned_estimate,
        lagrange_multiplier,
    )
    new_denoised = fine + update
    new_dual = lagrange_multiplier + fine - new_denoised
    return new_denoised, new_dual


def solution(mesh):
    placed = (
        P("views", ("groups", "space"), None, None),
        P("views", None, None, None),
        P("views", ("groups", "space"), None),
        P(("groups", "space", "views"), None, None),
        P(("groups", "space", "views"), None, None),
        P(),
        P(),
        P(),
        P(),
        P(),
        P(),
        P(),
    )
    return jax.shard_map(
        functools.partial(body, mesh.shape["space"]),
        mesh=mesh,
        in_specs=placed,
        out_specs=(
            P(("groups", "space", "views"), None, None),
            P(("groups", "space", "views"), None, None),
        ),
        check_vma=False,
    )
```

```python
import functools

import jax
import jax.numpy as jnp
from jax import lax
from jax.experimental import pallas as pl
from jax.experimental.pallas import tpu as pltpu
from jax.sharding import PartitionSpec as P

highest = lax.Precision.HIGHEST
step_size = 0.5
MESH = pl.DeviceIdType.MESH
f32 = jnp.float32
bf16 = jnp.bfloat16
RELATIONS = ((0, 1), (-1, 0), (-1, 1), (1, 0), (1, 1))


def halves(value):
    high = value.astype(bf16)
    low = (value - high.astype(f32)).astype(bf16)
    return high, low


def dot3(left, right):
    lh, ll = left
    rh, rl = right
    return (
        jnp.dot(lh, rh, preferred_element_type=f32)
        + jnp.dot(lh, rl, preferred_element_type=f32)
        + jnp.dot(ll, rh, preferred_element_type=f32)
    )


NT = (((1,), (1,)), ((), ()))
TN = (((0,), (0,)), ((), ()))


def dotg3(left, right, dims):
    lh, ll = left
    rh, rl = right
    total = None
    for first, second in ((lh, rh), (lh, rl), (ll, rh)):
        term = lax.dot_general(first, second, dims, preferred_element_type=f32)
        total = term if total is None else total + term
    return total


def thirds(value):
    high = value.astype(bf16)
    rest = value - high.astype(f32)
    middle = rest.astype(bf16)
    low = (rest - middle.astype(f32)).astype(bf16)
    return high, middle, low


def iota(shape, dim):
    return lax.broadcasted_iota(jnp.int32, shape, dim)


def row_of(scalars, count):
    lane = iota((1, 128), 1)
    row = jnp.zeros((1, 128), f32)
    for c in range(count):
        row = jnp.where(lane == c, scalars[c], row)
    return row[:, 0:count]


def kernel(
    space, taps_hbm, cover_hbm, final_hbm, gain_hbm, sharp_hbm, lift_hbm, weights_hbm,
    channel_hbm, back_hbm, images_hbm, cleaned_hbm, lagrange_hbm, update_out, fine_out,
    cover, final_in, gain_in, sharp_in, tap_rows, lift_in, weights_in, taps_in,
    back_in, images, cleaned, lagrange, field, wide, part, parts_in, rows_pad,
    y_forward, y_adjoint, z_rows, xz_forward, xz_adjoint, spreads, lift, lift_final, weights, channel_taps,
    stack, deviations, bands, conv, mixed, stats, gathered,
    local, send1, recv1, send2, recv2, send3, recv3,
):
    group = lax.axis_index("groups")
    s = lax.axis_index("space")
    w = lax.axis_index("views")
    me = 2 * s + w
    count = 2 * space

    loads = [
        pltpu.make_async_copy(cleaned_hbm, cleaned, local.at[0]),
        pltpu.make_async_copy(lagrange_hbm, lagrange, local.at[1]),
        pltpu.make_async_copy(taps_hbm, tap_rows, local.at[3]),
        pltpu.make_async_copy(images_hbm, images, local.at[4]),
        pltpu.make_async_copy(cover_hbm, cover, local.at[5]),
        pltpu.make_async_copy(final_hbm, final_in, local.at[6]),
        pltpu.make_async_copy(gain_hbm, gain_in, local.at[7]),
        pltpu.make_async_copy(sharp_hbm, sharp_in, local.at[8]),
        pltpu.make_async_copy(lift_hbm, lift_in, local.at[9]),
        pltpu.make_async_copy(weights_hbm, weights_in, local.at[10]),
        pltpu.make_async_copy(channel_hbm, taps_in, local.at[11]),
        pltpu.make_async_copy(back_hbm, back_in, local.at[12]),
    ]
    for load in loads:
        load.start()

    def present(ds):
        if ds < 0:
            return s > 0
        if ds > 0:
            return s < space - 1
        return s >= 0

    def other(flip):
        return 1 - w if flip else w

    def peer(step):
        return lax.rem(me + step, count)

    barrier = pltpu.get_barrier_semaphore()

    def greet(step, carry):
        to = peer(step)
        pl.semaphore_signal(
            barrier, inc=1, device_id=(group, to // 2, lax.rem(to, 2)), device_id_type=MESH
        )
        return carry

    lax.fori_loop(1, count, greet, 0)

    loads[0].wait()
    loads[1].wait()
    field[...] = cleaned[...] - lagrange[...]
    wide[pl.ds(16 + 8 * w, 8)] = field[...]
    wide[0:6] = jnp.zeros((6,) + wide.shape[1:], f32)
    wide[42:48] = jnp.zeros((6,) + wide.shape[1:], f32)

    @pl.when(s == 0)
    def _():
        wide[6:16] = jnp.zeros((10,) + wide.shape[1:], f32)

    @pl.when(s == space - 1)
    def _():
        wide[32:42] = jnp.zeros((10,) + wide.shape[1:], f32)

    pl.semaphore_wait(barrier, count - 1)

    def first(k, ds, flip, sender_w):
        begin, size = 0, 8
        if (ds, sender_w) == (1, 0):
            begin, size = 6, 2
        if (ds, sender_w) == (-1, 1):
            begin, size = 0, 2
        return pltpu.make_async_remote_copy(
            src_ref=field.at[pl.ds(begin, size)],
            dst_ref=wide.at[pl.ds(16 * (1 - ds) + 8 * sender_w + begin, size)],
            send_sem=send1.at[k],
            recv_sem=recv1.at[k],
            device_id=(group, s + ds, other(flip)),
            device_id_type=MESH,
        )

    for k, (ds, flip) in enumerate(RELATIONS):
        for core in range(2):

            @pl.when(present(ds) & (w == core))
            def _():
                first(k, ds, flip, core).start()

    for load in loads[2:]:
        load.wait()
    rows = iota((128, 128), 0)
    cols = iota((128, 128), 1)
    keep_y = jnp.abs(rows - cols) <= 10
    lane_tile = iota((8, 128), 1) // 16
    rows_pad[...] = jnp.zeros_like(rows_pad)
    rows_pad[:, :, :, 0:21] = tap_rows[...]

    def build_y(v, carry):
        for r in range(2):
            row = pltpu.roll(rows_pad[v, 1], 118, 1)[r : r + 1]
            spread = pltpu.roll(
                jnp.broadcast_to(row, (128, 128)), 0, 1, stride=1, stride_axis=0
            )
            high, low = halves(jnp.where(keep_y, spread, 0.0))
            for k, value in enumerate((high, high, low)):
                y_forward[v, :, 384 * r + 128 * k : 384 * r + 128 * k + 128] = value
                y_adjoint[v, 128 * k : 128 * k + 128, 128 * r : 128 * r + 128] = value
        return carry

    lax.fori_loop(0, images.shape[0], build_y, 0)

    taps_x = jnp.concatenate([rows_pad[v, 0] for v in range(4)], axis=0)
    taps_z = jnp.concatenate([rows_pad[v, 2] for v in range(4)], axis=0)
    tap = iota((128, 896), 0)
    spot_x = iota((128, 896), 1)
    wanted = jnp.where(spot_x < 384, spot_x // 8 - 6, 35 - (spot_x - 384) // 8)
    select_x = jnp.where((tap == wanted) & (tap < 21), 1.0, 0.0)
    tap = iota((128, 1024), 0)
    spot_z = iota((128, 1024), 1)
    distance = lax.rem(spot_z, 8) - spot_z // 128
    bases_x = jnp.dot(taps_x, select_x, precision=highest, preferred_element_type=f32)
    for mirrored in range(2):
        wanted = 10 - distance if mirrored else 10 + distance
        found = jnp.dot(
            taps_z,
            jnp.where(tap == wanted, 1.0, 0.0),
            precision=highest,
            preferred_element_type=f32,
        )
        for z in range(8):
            z_rows[8 * mirrored + z] = found[:, 128 * z : 128 * z + 128]

    for vr in range(8):
        pattern = z_rows[0:8, vr, :]
        base = jnp.concatenate([pattern] * 3, axis=1) * bases_x[vr : vr + 1, 0:384]
        for x in range(0, 16, 2):
            pair = [pltpu.roll(base, 8 * x, 1) if x else base, pltpu.roll(base, 8 * x + 8, 1)]
            high, low = halves(jnp.concatenate(pair, axis=0))
            at = 128 * vr + 8 * x
            xz_forward[at : at + 16, 0:384] = high
            xz_forward[at : at + 16, 384:768] = low
        pattern = z_rows[8:16, vr, :]
        base = jnp.concatenate([pattern] * 4, axis=1) * bases_x[vr : vr + 1, 384:896]
        for p in range(0, 36, 2):
            pair = []
            for q in (p, p + 1):
                begin = 8 * (35 - q)
                pair.append(base[:, begin : begin + 128])
            high, low = halves(jnp.concatenate(pair, axis=0))
            xz_adjoint[0, 8 * p : 8 * p + 16, 128 * vr : 128 * vr + 128] = high
            xz_adjoint[1, 8 * p : 8 * p + 16, 128 * vr : 128 * vr + 128] = low

    for k, (ds, flip) in enumerate(RELATIONS):
        for core in range(2):

            @pl.when(present(ds) & (w == core))
            def _():
                first(k, ds, flip, core).wait_send()

            @pl.when(present(-ds) & (other(flip) == core))
            def _():
                first(k, ds, flip, core).wait_recv()

    high, low = halves(wide[...].reshape(384, 128))
    field_stack = jnp.concatenate([high, low, high], axis=0)
    for v in range(4):
        along_xz = xz_forward[256 * v : 256 * v + 256, :]
        along_xz = jnp.concatenate([along_xz[:, 0:384], along_xz], axis=1)
        moved = jnp.dot(along_xz, field_stack, preferred_element_type=f32)
        pieces = []
        for r in range(2):
            high, low = halves(moved[128 * r : 128 * r + 128])
            pieces += [high, low, high]
        evolved = lax.dot_general(
            jnp.concatenate(pieces, axis=1), y_forward[v], NT, preferred_element_type=f32
        )
        mask = jnp.zeros((8, 128), f32)
        for j in range(8):
            mask = jnp.where(lane_tile == j, cover[v, 0, j].astype(f32), mask)
        residual = (evolved.reshape(16, 8, 128) - images[v].astype(f32)) * mask[None]
        high, low = halves(residual.reshape(128, 128))
        spread = jnp.dot(
            jnp.concatenate([high, low, high], axis=1), y_adjoint[v], preferred_element_type=f32
        )
        for r in range(2):
            high, low = halves(spread[:, 128 * r : 128 * r + 128])
            at = 256 * v + 128 * r
            spreads[at : at + 128, 0:128] = high
            spreads[at : at + 128, 128:256] = low
    both = jnp.dot(xz_adjoint[0], spreads[...], preferred_element_type=f32)
    both = both[:, 0:128] + both[:, 128:256]
    both = both + jnp.dot(xz_adjoint[1], spreads[:, 0:128], preferred_element_type=f32)
    part[8:44] = both.reshape(36, 8, 128)

    def second(k, ds, flip, target):
        begin, size = 0, 12
        if (ds, target) == (-1, 0):
            begin, size = 8, 4
        if (ds, target) == (1, 1):
            begin, size = 0, 4
        return pltpu.make_async_remote_copy(
            src_ref=part.at[pl.ds(8 * target + 16 + 16 * ds + begin, size)],
            dst_ref=parts_in.at[k, pl.ds(begin, size)],
            send_sem=send2.at[k],
            recv_sem=recv2.at[k],
            device_id=(group, s + ds, target),
            device_id_type=MESH,
        )

    for k, (ds, flip) in enumerate(RELATIONS):
        for core in range(2):

            @pl.when(present(ds) & (other(flip) == core))
            def _():
                second(k, ds, flip, core).start()

        @pl.when(jnp.logical_not(present(-ds)))
        def _():
            parts_in[k] = jnp.zeros(parts_in.shape[1:], f32)

        if ds == -1:

            @pl.when(present(1) & (w == 0))
            def _():
                parts_in[k, 0:8] = jnp.zeros((8,) + parts_in.shape[2:], f32)

        if ds == 1:

            @pl.when(present(-1) & (w == 1))
            def _():
                parts_in[k, 4:12] = jnp.zeros((8,) + parts_in.shape[2:], f32)

    final_row = row_of(final_in, 48)
    gain_row = row_of(gain_in, 48)
    row48 = iota((48, 48), 0)
    col48 = iota((48, 48), 1)
    gain = jnp.sum(jnp.where(row48 == col48, gain_row, 0.0), axis=1, keepdims=True)
    gain_wide = jnp.broadcast_to(gain, (48, 1280))
    kernel_t = lift_in[...]
    centred = thirds(kernel_t - jnp.sum(kernel_t, axis=1, keepdims=True) * (1.0 / 48.0))
    mapped = thirds(
        jnp.broadcast_to(jnp.sum(kernel_t * final_row, axis=1, keepdims=True), (27, 16))
    )
    spot = iota((27, 512), 1)
    segment = spot // 80
    inner = lax.rem(spot, 80)
    sub = lax.rem(inner, 8)
    start_tap = 9 * (lax.rem(inner, 24) // 8) + inner // 24
    row16 = iota((16, 512), 0)
    lift_final[...] = jnp.zeros_like(lift_final)

    def build_lift(z, carry):
        step = sub - z + 1
        fits = (step >= 0) & (step <= 2) & (inner < 72)
        fits = fits & (iota((27, 512), 0) == start_tap + 3 * step)
        tables = (
            jnp.where(fits & ((segment <= 1) | (segment == 4)), 1.0, 0.0).astype(bf16),
            jnp.where(fits & ((segment == 2) | (segment == 3)), 1.0, 0.0).astype(bf16),
            jnp.where(fits & (segment == 5), 1.0, 0.0).astype(bf16),
        )

        def expand(pieces):
            total = None
            for piece, table in zip(pieces, tables):
                term = lax.dot_general(piece, table, TN, preferred_element_type=f32)
                total = term if total is None else total + term
            return total.astype(bf16)

        lift[z] = expand(centred)
        here = jnp.where(row16 == z, expand(mapped).astype(f32), 0.0)
        lift_final[...] = (lift_final[...].astype(f32) + here).astype(bf16)
        return carry

    lax.fori_loop(0, 8, build_lift, 0)
    eye48 = jnp.where(row48 == col48, 1.0, 0.0)
    weights[...] = lax.dot_general(
        weights_in[...], eye48.astype(bf16), TN, preferred_element_type=f32
    ).astype(bf16)
    eye27 = jnp.where(iota((27, 128), 0) == iota((27, 128), 1), 1.0, 0.0)
    channel_taps[...] = lax.dot_general(
        taps_in[...], eye27, TN, precision=highest, preferred_element_type=f32
    )
    back = jnp.dot(
        final_row, back_in[...].astype(f32), precision=highest, preferred_element_type=f32
    )

    split_taps = jnp.concatenate(halves(channel_taps[...][:, 0:27]), axis=0)
    spot_c = iota((27, 576), 1)
    shift = spot_c // 64
    plane_in = lax.rem(spot_c, 64) // 8
    tap_of = 9 * lax.rem(shift, 3) + shift // 3
    own = lax.rem(iota((8, 576), 1), 8) == iota((8, 576), 0)

    def build_conv(zz, carry):
        tiles = []
        for half in range(2):
            step = plane_in - (2 * zz + half) + 1
            fits = (step >= 0) & (step <= 2) & (iota((27, 576), 0) == tap_of + 3 * step)
            tiles.append(
                jnp.dot(
                    split_taps, jnp.where(fits, 1.0, 0.0).astype(bf16), preferred_element_type=f32
                )
            )
        at = pl.multiple_of(16 * zz, 16)
        for g in range(18):
            for part_of in range(2):
                row = 144 * part_of + 8 * g
                pair = [jnp.where(own, tile[row : row + 8], 0.0) for tile in tiles]
                conv[g, pl.ds(64 * part_of + at, 16), :] = jnp.concatenate(pair, axis=0).astype(
                    bf16
                )
        return carry

    lax.fori_loop(0, 4, build_conv, 0)

    for k, (ds, flip) in enumerate(RELATIONS):
        for core in range(2):

            @pl.when(present(ds) & (other(flip) == core))
            def _():
                second(k, ds, flip, core).wait_send()

            @pl.when(present(-ds) & (w == core))
            def _():
                second(k, ds, flip, core).wait_recv()

    gradient = part[pl.ds(8 * w + 16, 12)]
    for k in range(5):
        gradient = gradient + parts_in[k]
    fine = wide[pl.ds(14 + 8 * w, 12)] - step_size * gradient
    row_id = 16 * s + 8 * w - 2 + iota(fine.shape, 0)
    fine = jnp.where((row_id >= 0) & (row_id < 16 * space), fine, 0.0)
    fine_out[...] = fine[2:10]

    lane3 = iota(fine.shape, 2)
    before = jnp.where(lane3 == 0, 0.0, pltpu.roll(fine, 1, 2))
    after = jnp.where(lane3 == 127, 0.0, pltpu.roll(fine, 127, 2))
    for x in range(10):
        pieces = []
        for moved in (before, fine, after):
            pieces.append(moved[x : x + 3].reshape(24, 128))
        pieces.append(jnp.zeros((8, 128), f32))
        high, middle, low = thirds(jnp.concatenate(pieces, axis=0))
        at = slice(x * 128, (x + 1) * 128)
        for k, piece in enumerate((high, middle, high, middle, low, high)):
            stack[80 * k : 80 * k + 80, at] = piece
    stack[480:512] = jnp.zeros((32, 1280), bf16)
    update = jnp.dot(lift_final[...], stack[...], preferred_element_type=f32)

    wide_row = 16 * s + 8 * w - 1 + iota((48, 1280), 1) // 128
    inside = (wide_row >= 0) & (wide_row < 16 * space)

    deviations[...] = jnp.dot(
        lift[...].reshape(384, 512), stack[...], preferred_element_type=f32
    ).reshape(8, 48, 1280)

    lane16 = iota((16, 128), 1)

    def plane_pair(zz, carry):
        pair = []
        for half in range(2):
            dev = deviations[2 * zz + half]
            spread = jnp.sum(dev * dev, axis=0, keepdims=True) * (1.0 / 48.0)
            value = jnp.where(inside, dev * lax.rsqrt(spread + 1e-05) * gain_wide, 0.0)
            pair.append(jnp.dot(weights[...], value.astype(bf16), preferred_element_type=f32))
        rows = pl.ds(pl.multiple_of(16 * zz, 16), 16)
        for g in range(18):
            for x in range(10):
                at = slice(x * 128, (x + 1) * 128)
                cell = jnp.concatenate([proj[8 * g : 8 * g + 8, at] for proj in pair], axis=0)
                bands[0, g, rows, at] = jnp.where(lane16 == 0, 0.0, pltpu.roll(cell, 1, 1)).astype(
                    bf16
                )
                bands[1, g, rows, at] = cell.astype(bf16)
                bands[2, g, rows, at] = jnp.where(
                    lane16 == 127, 0.0, pltpu.roll(cell, 127, 1)
                ).astype(bf16)
        return carry

    lax.fori_loop(0, 4, plane_pair, 0)

    def channel_group(g, carry):
        at = pl.multiple_of(g * 8, 8)
        for n in range(4):
            pieces = []
            for dy in range(3):
                for dx in range(3):
                    begin = dx * 128 + n * 256
                    pieces.append(bands[dy, g, :, begin : begin + 256])
            both = jnp.dot(
                conv[g], jnp.concatenate(pieces, axis=0), preferred_element_type=f32
            )
            total = both[0:64] + both[64:128]
            for z in range(8):
                mixed[z, pl.ds(at, 8), n * 256 : (n + 1) * 256] = total[8 * z : 8 * z + 8]
        return carry

    lax.fori_loop(0, 12, channel_group, 0)

    def gram_step(z, total):
        value = mixed[z, 0:96].astype(bf16)
        return total + lax.dot_general(value, value, NT, preferred_element_type=f32)

    gram = lax.fori_loop(0, 8, gram_step, jnp.zeros((96, 96), f32), unroll=True)

    same = row48 // 12 == col48 // 12
    block = jnp.where(same, 1.0, 0.0)
    row16 = iota((16, 48), 0)
    col16 = iota((16, 48), 1)
    pick = jnp.where(lax.rem(col16, 12) == row16, 1.0, 0.0)
    kq = jnp.where(same, gram[48:96, 0:48], 0.0)
    squares_q = jnp.sum(jnp.where(row48 == col48, gram[0:48, 0:48], 0.0), axis=0, keepdims=True)
    squares_k = jnp.sum(jnp.where(row48 == col48, gram[48:96, 48:96], 0.0), axis=0, keepdims=True)
    packed = jnp.dot(pick, kq, precision=highest, preferred_element_type=f32)
    packed = jnp.where(row16 == 12, squares_q, packed)
    packed = jnp.where(row16 == 13, squares_k, packed)
    stats[...] = jnp.zeros_like(stats)
    stats[:, 0:48] = packed[0:8]
    stats[:, 64:112] = packed[8:16]

    def share(step):
        to = peer(step)
        return pltpu.make_async_remote_copy(
            src_ref=stats,
            dst_ref=gathered.at[step],
            send_sem=send3.at[step],
            recv_sem=recv3.at[step],
            device_id=(group, to // 2, lax.rem(to, 2)),
            device_id_type=MESH,
        )

    def start(step, carry):
        share(step).start()
        return carry

    def finish(step, carry):
        share(step).wait()
        return carry

    lax.fori_loop(1, count, start, 0)
    gathered[0] = stats[...]
    lax.fori_loop(12, 18, channel_group, 0)
    lax.fori_loop(1, count, finish, 0)

    def add(step, total):
        slot = lax.rem(me - step + count, count)
        return total + gathered[slot]

    paired = lax.fori_loop(0, count, add, jnp.zeros((8, 128), f32))
    summed = jnp.concatenate([paired[:, 0:48], paired[:, 64:112]], axis=0)
    squares_q = summed[12:13]
    squares_k = summed[13:14]
    lengths_k = jnp.dot(
        pick * jnp.sqrt(squares_k + 1e-06), block, precision=highest, preferred_element_type=f32
    )
    valid = row16 < 12
    head = iota((1, 48), 1) // 12
    sharp_row = jnp.zeros((1, 48), f32)
    for h in range(4):
        sharp_row = jnp.where(head == h, sharp_in[h], sharp_row)
    logits = sharp_row * summed / (jnp.sqrt(squares_q + 1e-06) * jnp.where(valid, lengths_k, 1.0))
    raised = jnp.where(valid, jnp.exp(jnp.where(valid, logits, 0.0)), 0.0)
    shares = (raised / jnp.sum(raised, axis=0, keepdims=True)).astype(bf16).astype(f32)
    placed_shares = lax.dot_general(
        shares, pick, TN, precision=highest, preferred_element_type=f32
    )
    placed_shares = jnp.where(same, placed_shares, 0.0).astype(bf16)
    back_high, back_low = halves(back)

    def value_plane(z, total):
        attended = jnp.dot(
            placed_shares, mixed[z, 96:144].astype(bf16), preferred_element_type=f32
        )
        back_rows = jnp.where(row16 == z, back_high.astype(f32), 0.0)
        back_rows = jnp.where(row16 == z + 8, back_low.astype(f32), back_rows)
        return total + jnp.dot(
            back_rows.astype(bf16), attended.astype(bf16), preferred_element_type=f32
        )

    added = lax.fori_loop(0, 8, value_plane, jnp.zeros((16, 1024), f32), unroll=True)
    extra = added[0:8] + added[8:16]
    for x in range(8):
        update_out[x] = (
            update[0:8, (x + 1) * 128 : (x + 2) * 128] + extra[:, x * 128 : (x + 1) * 128]
        )


def body(
    space,
    acquired_images,
    blur_profile_coefficients,
    specimen_coverage,
    cleaned_estimate,
    lagrange_multiplier,
    lifting_kernel,
    standardize_factor,
    triple_lifting_kernel,
    per_channel_kernel,
    sharpness_factor,
    mixing_back_kernel,
    final_mapping_kernel,
):
    vmem = pl.BlockSpec(memory_space=pltpu.VMEM)
    hbm = pl.BlockSpec(memory_space=pltpu.HBM)
    profiles = blur_profile_coefficients.transpose(0, 2, 1, 3)
    count = 2 * space
    shape = pltpu.VMEM((8, 8, 128), f32)
    dma = pltpu.SemaphoreType.DMA
    update, fine = pl.pallas_call(
        functools.partial(kernel, space),
        out_shape=(shape, shape),
        in_specs=[hbm] * 12,
        out_specs=(vmem, vmem),
        scratch_shapes=[
            pltpu.SMEM((4, 1, 8), jnp.int32),
            pltpu.SMEM((48,), f32),
            pltpu.SMEM((48,), f32),
            pltpu.SMEM((4,), f32),
            pltpu.VMEM((4, 3, 2, 21), f32),
            pltpu.VMEM((27, 48), f32),
            pltpu.VMEM((48, 144), bf16),
            pltpu.VMEM((27, 144), f32),
            pltpu.VMEM((48, 48), bf16),
            pltpu.VMEM((4, 16, 8, 128), bf16),
            pltpu.VMEM((8, 8, 128), f32),
            pltpu.VMEM((8, 8, 128), f32),
            pltpu.VMEM((8, 8, 128), f32),
            pltpu.VMEM((48, 8, 128), f32),
            pltpu.VMEM((52, 8, 128), f32),
            pltpu.VMEM((5, 12, 8, 128), f32),
            pltpu.VMEM((4, 3, 2, 128), f32),
            pltpu.VMEM((4, 128, 768), bf16),
            pltpu.VMEM((4, 384, 256), bf16),
            pltpu.VMEM((16, 8, 128), f32),
            pltpu.VMEM((1024, 768), bf16),
            pltpu.VMEM((2, 288, 1024), bf16),
            pltpu.VMEM((1024, 256), bf16),
            pltpu.VMEM((8, 48, 512), bf16),
            pltpu.VMEM((16, 512), bf16),
            pltpu.VMEM((144, 48), bf16),
            pltpu.VMEM((144, 128), f32),
            pltpu.VMEM((512, 1280), bf16),
            pltpu.VMEM((8, 48, 1280), f32),
            pltpu.VMEM((3, 18, 64, 1280), bf16),
            pltpu.VMEM((18, 128, 576), bf16),
            pltpu.VMEM((8, 144, 1024), f32),
            pltpu.VMEM((8, 128), f32),
            pltpu.VMEM((count, 8, 128), f32),
            dma((13,)),
            dma((5,)),
            dma((5,)),
            dma((5,)),
            dma((5,)),
            dma((count,)),
            dma((count,)),
        ],
        compiler_params=pltpu.CompilerParams(
            collective_id=0, has_side_effects=True, vmem_limit_bytes=66912256
        ),
        name="iteration",
    )(
        profiles,
        specimen_coverage,
        final_mapping_kernel,
        standardize_factor,
        sharpness_factor,
        lifting_kernel.T,
        triple_lifting_kernel.T,
        per_channel_kernel.T,
        mixing_back_kernel,
        acquired_images,
        cleaned_estimate,
        lagrange_multiplier,
    )
    new_denoised = fine + update
    new_dual = lagrange_multiplier + fine - new_denoised
    return new_denoised, new_dual


def solution(mesh):
    placed = (
        P("views", ("groups", "space"), None, None),
        P("views", None, None, None),
        P("views", ("groups", "space"), None),
        P(("groups", "space", "views"), None, None),
        P(("groups", "space", "views"), None, None),
        P(),
        P(),
        P(),
        P(),
        P(),
        P(),
        P(),
    )
    return jax.shard_map(
        functools.partial(body, mesh.shape["space"]),
        mesh=mesh,
        in_specs=placed,
        out_specs=(
            P(("groups", "space", "views"), None, None),
            P(("groups", "space", "views"), None, None),
        ),
        check_vma=False,
    )
```

```python
import functools

import jax
import jax.numpy as jnp
from jax import lax
from jax.experimental import pallas as pl
from jax.experimental.pallas import tpu as pltpu
from jax.sharding import PartitionSpec as P

highest = lax.Precision.HIGHEST
step_size = 0.5
MESH = pl.DeviceIdType.MESH
f32 = jnp.float32
bf16 = jnp.bfloat16
RELATIONS = ((0, 1), (-1, 0), (-1, 1), (1, 0), (1, 1))


def halves(value):
    high = value.astype(bf16)
    low = (value - high.astype(f32)).astype(bf16)
    return high, low


def dot3(left, right):
    lh, ll = left
    rh, rl = right
    return (
        jnp.dot(lh, rh, preferred_element_type=f32)
        + jnp.dot(lh, rl, preferred_element_type=f32)
        + jnp.dot(ll, rh, preferred_element_type=f32)
    )


NT = (((1,), (1,)), ((), ()))
TN = (((0,), (0,)), ((), ()))


def dotg3(left, right, dims):
    lh, ll = left
    rh, rl = right
    total = None
    for first, second in ((lh, rh), (lh, rl), (ll, rh)):
        term = lax.dot_general(first, second, dims, preferred_element_type=f32)
        total = term if total is None else total + term
    return total


def thirds(value):
    high = value.astype(bf16)
    rest = value - high.astype(f32)
    middle = rest.astype(bf16)
    low = (rest - middle.astype(f32)).astype(bf16)
    return high, middle, low


def iota(shape, dim):
    return lax.broadcasted_iota(jnp.int32, shape, dim)


def row_of(scalars, count):
    lane = iota((1, 128), 1)
    row = jnp.zeros((1, 128), f32)
    for c in range(count):
        row = jnp.where(lane == c, scalars[c], row)
    return row[:, 0:count]


def kernel(
    space, taps_hbm, cover_hbm, final_hbm, gain_hbm, sharp_hbm, lift_hbm, weights_hbm,
    channel_hbm, back_hbm, images_hbm, cleaned_hbm, lagrange_hbm, update_out, fine_out,
    cover, final_in, gain_in, sharp_in, tap_rows, lift_in, weights_in, taps_in,
    back_in, images, cleaned, lagrange, field, wide, part, parts_in, rows_pad,
    y_forward, y_adjoint, z_rows, xz_forward, xz_adjoint, spreads, lift, lift_final, weights, channel_taps,
    stack, deviations, bands, conv, mixed, stats, gathered,
    local, send1, recv1, send2, recv2, send3, recv3, ready,
):
    group = lax.axis_index("groups")
    s = lax.axis_index("space")
    w = lax.axis_index("views")
    me = 2 * s + w
    count = 2 * space

    loads = [
        pltpu.make_async_copy(cleaned_hbm, cleaned, local.at[0]),
        pltpu.make_async_copy(lagrange_hbm, lagrange, local.at[1]),
        pltpu.make_async_copy(taps_hbm, tap_rows, local.at[3]),
        pltpu.make_async_copy(images_hbm, images, local.at[4]),
        pltpu.make_async_copy(cover_hbm, cover, local.at[5]),
        pltpu.make_async_copy(final_hbm, final_in, local.at[6]),
        pltpu.make_async_copy(gain_hbm, gain_in, local.at[7]),
        pltpu.make_async_copy(sharp_hbm, sharp_in, local.at[8]),
        pltpu.make_async_copy(lift_hbm, lift_in, local.at[9]),
        pltpu.make_async_copy(weights_hbm, weights_in, local.at[10]),
        pltpu.make_async_copy(channel_hbm, taps_in, local.at[11]),
        pltpu.make_async_copy(back_hbm, back_in, local.at[12]),
    ]
    for load in loads:
        load.start()

    def present(ds):
        if ds < 0:
            return s > 0
        if ds > 0:
            return s < space - 1
        return s >= 0

    def other(flip):
        return 1 - w if flip else w

    def peer(step):
        return lax.rem(me + step, count)

    barrier = pltpu.get_barrier_semaphore()

    for ds, flip in RELATIONS:

        @pl.when(present(ds))
        def _():
            pl.semaphore_signal(
                barrier, inc=1, device_id=(group, s + ds, other(flip)), device_id_type=MESH
            )

    loads[0].wait()
    loads[1].wait()
    field[...] = cleaned[...] - lagrange[...]
    wide[pl.ds(16 + 8 * w, 8)] = field[...]
    wide[0:6] = jnp.zeros((6,) + wide.shape[1:], f32)
    wide[42:48] = jnp.zeros((6,) + wide.shape[1:], f32)

    @pl.when(s == 0)
    def _():
        wide[6:16] = jnp.zeros((10,) + wide.shape[1:], f32)

    @pl.when(s == space - 1)
    def _():
        wide[32:42] = jnp.zeros((10,) + wide.shape[1:], f32)

    beside = 1 + 2 * present(-1).astype(jnp.int32) + 2 * present(1).astype(jnp.int32)
    pl.semaphore_wait(barrier, beside)

    spans = []
    while 2 << len(spans) < space - 1:
        spans.append(2 << len(spans))

    def tell(k):
        for side, at in enumerate((s - spans[k], s + spans[k])):

            @pl.when((at >= 0) & (at < space))
            def _():
                pl.semaphore_signal(
                    ready.at[k, 1 - side], inc=1, device_id=(group, at, w), device_id_type=MESH
                )

    def hear(k):
        for side, at in enumerate((s - spans[k], s + spans[k])):

            @pl.when((at >= 0) & (at < space))
            def _():
                pl.semaphore_wait(ready.at[k, side], 1)


    def first(k, ds, flip, sender_w):
        begin, size = 0, 8
        if (ds, sender_w) == (1, 0):
            begin, size = 6, 2
        if (ds, sender_w) == (-1, 1):
            begin, size = 0, 2
        return pltpu.make_async_remote_copy(
            src_ref=field.at[pl.ds(begin, size)],
            dst_ref=wide.at[pl.ds(16 * (1 - ds) + 8 * sender_w + begin, size)],
            send_sem=send1.at[k],
            recv_sem=recv1.at[k],
            device_id=(group, s + ds, other(flip)),
            device_id_type=MESH,
        )

    for k, (ds, flip) in enumerate(RELATIONS):
        for core in range(2):

            @pl.when(present(ds) & (w == core))
            def _():
                first(k, ds, flip, core).start()

    for load in loads[2:]:
        load.wait()
    rows = iota((128, 128), 0)
    cols = iota((128, 128), 1)
    keep_y = jnp.abs(rows - cols) <= 10
    lane_tile = iota((8, 128), 1) // 16
    rows_pad[...] = jnp.zeros_like(rows_pad)
    rows_pad[:, :, :, 0:21] = tap_rows[...]

    def build_y(v, carry):
        for r in range(2):
            row = pltpu.roll(rows_pad[v, 1], 118, 1)[r : r + 1]
            spread = pltpu.roll(
                jnp.broadcast_to(row, (128, 128)), 0, 1, stride=1, stride_axis=0
            )
            high, low = halves(jnp.where(keep_y, spread, 0.0))
            for k, value in enumerate((high, high, low)):
                y_forward[v, :, 384 * r + 128 * k : 384 * r + 128 * k + 128] = value
                y_adjoint[v, 128 * k : 128 * k + 128, 128 * r : 128 * r + 128] = value
        return carry

    lax.fori_loop(0, images.shape[0], build_y, 0, unroll=True)

    taps_x = jnp.concatenate([rows_pad[v, 0] for v in range(4)], axis=0)
    taps_z = jnp.concatenate([rows_pad[v, 2] for v in range(4)], axis=0)
    spot_x = iota((32, 896), 1)
    spot_z = iota((32, 1024), 1)
    distance = lax.rem(spot_z, 8) - spot_z // 128

    def picked(tap_values, wanted):
        rows_in = jnp.concatenate([piece[:, 0:32] for piece in thirds(tap_values)], axis=0)
        select = jnp.where(iota(wanted.shape, 0) == wanted, 1.0, 0.0).astype(bf16)
        found = jnp.dot(rows_in, select, preferred_element_type=f32)
        return found[0:8] + found[8:16] + found[16:24]

    bases_x = picked(
        taps_x, jnp.where(spot_x < 384, spot_x // 8 - 6, 35 - (spot_x - 384) // 8)
    )
    for mirrored in range(2):
        found = picked(taps_z, 10 - distance if mirrored else 10 + distance)
        for z in range(8):
            z_rows[8 * mirrored + z] = found[:, 128 * z : 128 * z + 128]

    for vr in range(8):
        pattern = z_rows[0:8, vr, :]
        base = jnp.concatenate([pattern] * 3, axis=1) * bases_x[vr : vr + 1, 0:384]
        for x in range(0, 16, 2):
            pair = [pltpu.roll(base, 8 * x, 1) if x else base, pltpu.roll(base, 8 * x + 8, 1)]
            high, low = halves(jnp.concatenate(pair, axis=0))
            at = 128 * vr + 8 * x
            xz_forward[at : at + 16, 0:384] = high
            xz_forward[at : at + 16, 384:768] = low
        pattern = z_rows[8:16, vr, :]
        base = jnp.concatenate([pattern] * 4, axis=1) * bases_x[vr : vr + 1, 384:896]
        for p in range(0, 36, 2):
            pair = []
            for q in (p, p + 1):
                begin = 8 * (35 - q)
                pair.append(base[:, begin : begin + 128])
            high, low = halves(jnp.concatenate(pair, axis=0))
            xz_adjoint[0, 8 * p : 8 * p + 16, 128 * vr : 128 * vr + 128] = high
            xz_adjoint[1, 8 * p : 8 * p + 16, 128 * vr : 128 * vr + 128] = low

    for k, (ds, flip) in enumerate(RELATIONS):
        for core in range(2):

            @pl.when(present(ds) & (w == core))
            def _():
                first(k, ds, flip, core).wait_send()

            @pl.when(present(-ds) & (other(flip) == core))
            def _():
                first(k, ds, flip, core).wait_recv()

    high, low = halves(wide[...].reshape(384, 128))
    field_stack = jnp.concatenate([high, low, high], axis=0)
    for v in range(4):
        along_xz = xz_forward[256 * v : 256 * v + 256, :]
        along_xz = jnp.concatenate([along_xz[:, 0:384], along_xz], axis=1)
        moved = jnp.dot(along_xz, field_stack, preferred_element_type=f32)
        pieces = []
        for r in range(2):
            high, low = halves(moved[128 * r : 128 * r + 128])
            pieces += [high, low, high]
        evolved = lax.dot_general(
            jnp.concatenate(pieces, axis=1), y_forward[v], NT, preferred_element_type=f32
        )
        mask = jnp.zeros((8, 128), f32)
        for j in range(8):
            mask = jnp.where(lane_tile == j, cover[v, 0, j].astype(f32), mask)
        residual = (evolved.reshape(16, 8, 128) - images[v].astype(f32)) * mask[None]
        high, low = halves(residual.reshape(128, 128))
        spread = jnp.dot(
            jnp.concatenate([high, low, high], axis=1), y_adjoint[v], preferred_element_type=f32
        )
        for r in range(2):
            high, low = halves(spread[:, 128 * r : 128 * r + 128])
            at = 256 * v + 128 * r
            spreads[at : at + 128, 0:128] = high
            spreads[at : at + 128, 128:256] = low
    both = jnp.dot(xz_adjoint[0], spreads[...], preferred_element_type=f32)
    both = both[:, 0:128] + both[:, 128:256]
    both = both + jnp.dot(xz_adjoint[1], spreads[:, 0:128], preferred_element_type=f32)
    part[8:44] = both.reshape(36, 8, 128)

    def second(k, ds, flip, target):
        begin, size = 0, 12
        if (ds, target) == (-1, 0):
            begin, size = 8, 4
        if (ds, target) == (1, 1):
            begin, size = 0, 4
        return pltpu.make_async_remote_copy(
            src_ref=part.at[pl.ds(8 * target + 16 + 16 * ds + begin, size)],
            dst_ref=parts_in.at[k, pl.ds(begin, size)],
            send_sem=send2.at[k],
            recv_sem=recv2.at[k],
            device_id=(group, s + ds, target),
            device_id_type=MESH,
        )

    for k, (ds, flip) in enumerate(RELATIONS):
        for core in range(2):

            @pl.when(present(ds) & (other(flip) == core))
            def _():
                second(k, ds, flip, core).start()

        @pl.when(jnp.logical_not(present(-ds)))
        def _():
            parts_in[k] = jnp.zeros(parts_in.shape[1:], f32)

        if ds == -1:

            @pl.when(present(1) & (w == 0))
            def _():
                parts_in[k, 0:8] = jnp.zeros((8,) + parts_in.shape[2:], f32)

        if ds == 1:

            @pl.when(present(-1) & (w == 1))
            def _():
                parts_in[k, 4:12] = jnp.zeros((8,) + parts_in.shape[2:], f32)

    final_row = row_of(final_in, 48)
    gain_row = row_of(gain_in, 48)
    row48 = iota((48, 48), 0)
    col48 = iota((48, 48), 1)
    gain = jnp.sum(jnp.where(row48 == col48, gain_row, 0.0), axis=1, keepdims=True)
    gain_wide = jnp.broadcast_to(gain, (48, 1280))
    kernel_t = lift_in[...]
    centred = thirds(kernel_t - jnp.sum(kernel_t, axis=1, keepdims=True) * (1.0 / 48.0))
    mapped = thirds(
        jnp.broadcast_to(jnp.sum(kernel_t * final_row, axis=1, keepdims=True), (27, 16))
    )
    pieces = []
    for main, side in zip(centred, mapped):
        pieces.append(jnp.concatenate([main.astype(f32), side.astype(f32)], axis=1))
        pieces.append(jnp.zeros((5, 64), f32))
    stacked = jnp.concatenate(pieces, axis=0).astype(bf16)
    eye96 = jnp.where(iota((96, 96), 0) == iota((96, 96), 1), 1.0, 0.0).astype(bf16)
    lift_rows = lax.dot_general(stacked, eye96, TN, preferred_element_type=f32).astype(bf16)
    spot = iota((96, 512), 1)
    segment = spot // 80
    inner = lax.rem(spot, 80)
    piece_of = jnp.where(
        (segment <= 1) | (segment == 4), 0, jnp.where(segment == 5, 2, 1)
    )
    table_tap = lax.rem(iota((96, 512), 0), 32)
    fits = (iota((96, 512), 0) // 32 == piece_of) & (inner < 72) & (spot < 480)
    fits = fits & (table_tap < 27) & (table_tap // 9 == lax.rem(inner, 24) // 8)
    fits = fits & (lax.rem(table_tap, 3) == inner // 24)
    plane_of = jnp.where(fits, lax.rem(inner, 8) - lax.rem(table_tap, 9) // 3 + 1, 99)
    row16 = iota((16, 512), 0)
    final_sum = jnp.zeros((16, 512), f32)
    for z in range(8):
        table = jnp.where(plane_of == z, 1.0, 0.0).astype(bf16)
        found = jnp.dot(lift_rows, table, preferred_element_type=f32)
        lift[z] = found[0:48].astype(bf16)
        final_sum = jnp.where(row16 == z, found[48:64], final_sum)
    lift_final[...] = final_sum.astype(bf16)

    eye48 = jnp.where(row48 == col48, 1.0, 0.0)
    weights[...] = lax.dot_general(
        weights_in[...], eye48.astype(bf16), TN, preferred_element_type=f32
    ).astype(bf16)
    eye27 = jnp.where(iota((27, 128), 0) == iota((27, 128), 1), 1.0, 0.0)
    channel_taps[...] = lax.dot_general(
        taps_in[...], eye27, TN, precision=highest, preferred_element_type=f32
    )
    back = jnp.dot(
        final_row, back_in[...].astype(f32), precision=highest, preferred_element_type=f32
    )

    split_taps = jnp.concatenate(halves(channel_taps[...][:, 0:32]), axis=0)
    spot_c = iota((32, 576), 1)
    shift = spot_c // 64
    conv_tap = iota((32, 576), 0)
    fits = (conv_tap < 27) & (conv_tap // 9 == lax.rem(shift, 3))
    fits = fits & (lax.rem(conv_tap, 3) == shift // 3)
    plane_of = jnp.where(fits, lax.rem(spot_c, 64) // 8 - lax.rem(conv_tap, 9) // 3 + 1, 99)
    own = lax.rem(iota((8, 576), 1), 8) == iota((8, 576), 0)
    for zz in range(4):
        tiles = []
        for half in range(2):
            table = jnp.where(plane_of == 2 * zz + half, 1.0, 0.0).astype(bf16)
            tiles.append(jnp.dot(split_taps, table, preferred_element_type=f32))
        for g in range(18):
            for part_of in range(2):
                row = 144 * part_of + 8 * g
                pair = [jnp.where(own, tile[row : row + 8], 0.0) for tile in tiles]
                at = 64 * part_of + 16 * zz
                conv[g, at : at + 16, :] = jnp.concatenate(pair, axis=0).astype(bf16)

    for k, (ds, flip) in enumerate(RELATIONS):
        for core in range(2):

            @pl.when(present(ds) & (other(flip) == core))
            def _():
                second(k, ds, flip, core).wait_send()

            @pl.when(present(-ds) & (w == core))
            def _():
                second(k, ds, flip, core).wait_recv()

    if spans:
        tell(0)

    gradient = part[pl.ds(8 * w + 16, 12)]
    for k in range(5):
        gradient = gradient + parts_in[k]
    fine = wide[pl.ds(14 + 8 * w, 12)] - step_size * gradient
    row_id = 16 * s + 8 * w - 2 + iota(fine.shape, 0)
    fine = jnp.where((row_id >= 0) & (row_id < 16 * space), fine, 0.0)
    fine_out[...] = fine[2:10]

    lane3 = iota(fine.shape, 2)
    before = jnp.where(lane3 == 0, 0.0, pltpu.roll(fine, 1, 2))
    after = jnp.where(lane3 == 127, 0.0, pltpu.roll(fine, 127, 2))
    for x in range(10):
        pieces = []
        for moved in (before, fine, after):
            pieces.append(moved[x : x + 3].reshape(24, 128))
        pieces.append(jnp.zeros((8, 128), f32))
        high, middle, low = thirds(jnp.concatenate(pieces, axis=0))
        at = slice(x * 128, (x + 1) * 128)
        for k, piece in enumerate((high, middle, high, middle, low, high)):
            stack[80 * k : 80 * k + 80, at] = piece
    stack[480:512] = jnp.zeros((32, 1280), bf16)
    update = jnp.dot(lift_final[...], stack[...], preferred_element_type=f32)

    wide_row = 16 * s + 8 * w - 1 + iota((48, 1280), 1) // 128
    inside = (wide_row >= 0) & (wide_row < 16 * space)

    deviations[...] = jnp.dot(
        lift[...].reshape(384, 512), stack[...], preferred_element_type=f32
    ).reshape(8, 48, 1280)

    lane16 = iota((16, 128), 1)

    def plane_pair(zz, carry):
        pair = []
        for half in range(2):
            dev = deviations[2 * zz + half]
            spread = jnp.sum(dev * dev, axis=0, keepdims=True) * (1.0 / 48.0)
            value = jnp.where(inside, dev * lax.rsqrt(spread + 1e-05) * gain_wide, 0.0)
            pair.append(jnp.dot(weights[...], value.astype(bf16), preferred_element_type=f32))
        rows = pl.ds(pl.multiple_of(16 * zz, 16), 16)
        for g in range(18):
            for x in range(10):
                at = slice(x * 128, (x + 1) * 128)
                cell = jnp.concatenate([proj[8 * g : 8 * g + 8, at] for proj in pair], axis=0)
                bands[0, g, rows, at] = jnp.where(lane16 == 0, 0.0, pltpu.roll(cell, 1, 1)).astype(
                    bf16
                )
                bands[1, g, rows, at] = cell.astype(bf16)
                bands[2, g, rows, at] = jnp.where(
                    lane16 == 127, 0.0, pltpu.roll(cell, 127, 1)
                ).astype(bf16)
        return carry

    lax.fori_loop(0, 4, plane_pair, 0, unroll=4)

    if spans:
        hear(0)
    if len(spans) > 1:
        tell(1)

    def channel_group(g, carry):
        at = pl.multiple_of(g * 8, 8)
        for n in range(4):
            pieces = []
            for dy in range(3):
                for dx in range(3):
                    begin = dx * 128 + n * 256
                    pieces.append(bands[dy, g, :, begin : begin + 256])
            both = jnp.dot(
                conv[g], jnp.concatenate(pieces, axis=0), preferred_element_type=f32
            )
            total = both[0:64] + both[64:128]
            for z in range(8):
                mixed[z, pl.ds(at, 8), n * 256 : (n + 1) * 256] = total[8 * z : 8 * z + 8]
        return carry

    lax.fori_loop(0, 12, channel_group, 0, unroll=6)

    def gram_step(z, total):
        value = mixed[z, 0:96].astype(bf16)
        return total + lax.dot_general(value, value, NT, preferred_element_type=f32)

    gram = lax.fori_loop(0, 8, gram_step, jnp.zeros((96, 96), f32), unroll=True)

    same = row48 // 12 == col48 // 12
    block = jnp.where(same, 1.0, 0.0)
    row16 = iota((16, 48), 0)
    col16 = iota((16, 48), 1)
    pick = jnp.where(lax.rem(col16, 12) == row16, 1.0, 0.0)
    kq = jnp.where(same, gram[48:96, 0:48], 0.0)
    squares_q = jnp.sum(jnp.where(row48 == col48, gram[0:48, 0:48], 0.0), axis=0, keepdims=True)
    squares_k = jnp.sum(jnp.where(row48 == col48, gram[48:96, 48:96], 0.0), axis=0, keepdims=True)
    packed = jnp.dot(pick, kq, precision=highest, preferred_element_type=f32)
    packed = jnp.where(row16 == 12, squares_q, packed)
    packed = jnp.where(row16 == 13, squares_k, packed)
    stats[...] = jnp.zeros_like(stats)
    stats[:, 0:48] = packed[0:8]
    stats[:, 64:112] = packed[8:16]

    for k in range(1, len(spans)):
        if k > 1:
            tell(k)
        hear(k)

    def share(step):
        to = peer(step)
        return pltpu.make_async_remote_copy(
            src_ref=stats,
            dst_ref=gathered.at[step],
            send_sem=send3.at[step],
            recv_sem=recv3.at[step],
            device_id=(group, to // 2, lax.rem(to, 2)),
            device_id_type=MESH,
        )

    def start(step, carry):
        share(step).start()
        return carry

    def finish(step, carry):
        share(step).wait()
        return carry

    lax.fori_loop(1, count, start, 0)
    gathered[0] = stats[...]
    lax.fori_loop(12, 18, channel_group, 0, unroll=6)
    lax.fori_loop(1, count, finish, 0)

    def add(step, total):
        slot = lax.rem(me - step + count, count)
        return total + gathered[slot]

    paired = lax.fori_loop(0, count, add, jnp.zeros((8, 128), f32))
    summed = jnp.concatenate([paired[:, 0:48], paired[:, 64:112]], axis=0)
    squares_q = summed[12:13]
    squares_k = summed[13:14]
    lengths_k = jnp.dot(
        pick * jnp.sqrt(squares_k + 1e-06), block, precision=highest, preferred_element_type=f32
    )
    valid = row16 < 12
    head = iota((1, 48), 1) // 12
    sharp_row = jnp.zeros((1, 48), f32)
    for h in range(4):
        sharp_row = jnp.where(head == h, sharp_in[h], sharp_row)
    logits = sharp_row * summed / (jnp.sqrt(squares_q + 1e-06) * jnp.where(valid, lengths_k, 1.0))
    raised = jnp.where(valid, jnp.exp(jnp.where(valid, logits, 0.0)), 0.0)
    shares = (raised / jnp.sum(raised, axis=0, keepdims=True)).astype(bf16).astype(f32)
    placed_shares = lax.dot_general(
        shares, pick, TN, precision=highest, preferred_element_type=f32
    )
    placed_shares = jnp.where(same, placed_shares, 0.0).astype(bf16)
    back_high, back_low = halves(back)

    def value_plane(z, total):
        attended = jnp.dot(
            placed_shares, mixed[z, 96:144].astype(bf16), preferred_element_type=f32
        )
        back_rows = jnp.where(row16 == z, back_high.astype(f32), 0.0)
        back_rows = jnp.where(row16 == z + 8, back_low.astype(f32), back_rows)
        return total + jnp.dot(
            back_rows.astype(bf16), attended.astype(bf16), preferred_element_type=f32
        )

    added = lax.fori_loop(0, 8, value_plane, jnp.zeros((16, 1024), f32), unroll=True)
    extra = added[0:8] + added[8:16]
    for x in range(8):
        update_out[x] = (
            update[0:8, (x + 1) * 128 : (x + 2) * 128] + extra[:, x * 128 : (x + 1) * 128]
        )


def body(
    space,
    acquired_images,
    blur_profile_coefficients,
    specimen_coverage,
    cleaned_estimate,
    lagrange_multiplier,
    lifting_kernel,
    standardize_factor,
    triple_lifting_kernel,
    per_channel_kernel,
    sharpness_factor,
    mixing_back_kernel,
    final_mapping_kernel,
):
    vmem = pl.BlockSpec(memory_space=pltpu.VMEM)
    hbm = pl.BlockSpec(memory_space=pltpu.HBM)
    profiles = blur_profile_coefficients.transpose(0, 2, 1, 3)
    count = 2 * space
    shape = pltpu.VMEM((8, 8, 128), f32)
    dma = pltpu.SemaphoreType.DMA
    update, fine = pl.pallas_call(
        functools.partial(kernel, space),
        out_shape=(shape, shape),
        in_specs=[hbm] * 12,
        out_specs=(vmem, vmem),
        scratch_shapes=[
            pltpu.SMEM((4, 1, 8), jnp.int32),
            pltpu.SMEM((48,), f32),
            pltpu.SMEM((48,), f32),
            pltpu.SMEM((4,), f32),
            pltpu.VMEM((4, 3, 2, 21), f32),
            pltpu.VMEM((27, 48), f32),
            pltpu.VMEM((48, 144), bf16),
            pltpu.VMEM((27, 144), f32),
            pltpu.VMEM((48, 48), bf16),
            pltpu.VMEM((4, 16, 8, 128), bf16),
            pltpu.VMEM((8, 8, 128), f32),
            pltpu.VMEM((8, 8, 128), f32),
            pltpu.VMEM((8, 8, 128), f32),
            pltpu.VMEM((48, 8, 128), f32),
            pltpu.VMEM((52, 8, 128), f32),
            pltpu.VMEM((5, 12, 8, 128), f32),
            pltpu.VMEM((4, 3, 2, 128), f32),
            pltpu.VMEM((4, 128, 768), bf16),
            pltpu.VMEM((4, 384, 256), bf16),
            pltpu.VMEM((16, 8, 128), f32),
            pltpu.VMEM((1024, 768), bf16),
            pltpu.VMEM((2, 288, 1024), bf16),
            pltpu.VMEM((1024, 256), bf16),
            pltpu.VMEM((8, 48, 512), bf16),
            pltpu.VMEM((16, 512), bf16),
            pltpu.VMEM((144, 48), bf16),
            pltpu.VMEM((144, 128), f32),
            pltpu.VMEM((512, 1280), bf16),
            pltpu.VMEM((8, 48, 1280), f32),
            pltpu.VMEM((3, 18, 64, 1280), bf16),
            pltpu.VMEM((18, 128, 576), bf16),
            pltpu.VMEM((8, 144, 1024), f32),
            pltpu.VMEM((8, 128), f32),
            pltpu.VMEM((count, 8, 128), f32),
            dma((13,)),
            dma((5,)),
            dma((5,)),
            dma((5,)),
            dma((5,)),
            dma((count,)),
            dma((count,)),
            pltpu.SemaphoreType.REGULAR((8, 2)),
        ],
        compiler_params=pltpu.CompilerParams(
            collective_id=0, has_side_effects=True, vmem_limit_bytes=66912256
        ),
        name="iteration",
    )(
        profiles,
        specimen_coverage,
        final_mapping_kernel,
        standardize_factor,
        sharpness_factor,
        lifting_kernel.T,
        triple_lifting_kernel.T,
        per_channel_kernel.T,
        mixing_back_kernel,
        acquired_images,
        cleaned_estimate,
        lagrange_multiplier,
    )
    new_denoised = fine + update
    new_dual = lagrange_multiplier + fine - new_denoised
    return new_denoised, new_dual


def solution(mesh):
    placed = (
        P("views", ("groups", "space"), None, None),
        P("views", None, None, None),
        P("views", ("groups", "space"), None),
        P(("groups", "space", "views"), None, None),
        P(("groups", "space", "views"), None, None),
        P(),
        P(),
        P(),
        P(),
        P(),
        P(),
        P(),
    )
    return jax.shard_map(
        functools.partial(body, mesh.shape["space"]),
        mesh=mesh,
        in_specs=placed,
        out_specs=(
            P(("groups", "space", "views"), None, None),
            P(("groups", "space", "views"), None, None),
        ),
        check_vma=False,
    )
```

```python
import functools

import jax
import jax.numpy as jnp
from jax import lax
from jax.experimental import pallas as pl
from jax.experimental.pallas import tpu as pltpu
from jax.sharding import PartitionSpec as P

highest = lax.Precision.HIGHEST
step_size = 0.5
MESH = pl.DeviceIdType.MESH
f32 = jnp.float32
bf16 = jnp.bfloat16
RELATIONS = ((-1, 0), (-1, 1), (1, 0), (1, 1), (0, 1))


def halves(value):
    high = value.astype(bf16)
    low = (value - high.astype(f32)).astype(bf16)
    return high, low


def dot3(left, right):
    lh, ll = left
    rh, rl = right
    return (
        jnp.dot(lh, rh, preferred_element_type=f32)
        + jnp.dot(lh, rl, preferred_element_type=f32)
        + jnp.dot(ll, rh, preferred_element_type=f32)
    )


NT = (((1,), (1,)), ((), ()))
TN = (((0,), (0,)), ((), ()))


def dotg3(left, right, dims):
    lh, ll = left
    rh, rl = right
    total = None
    for first, second in ((lh, rh), (lh, rl), (ll, rh)):
        term = lax.dot_general(first, second, dims, preferred_element_type=f32)
        total = term if total is None else total + term
    return total


def thirds(value):
    high = value.astype(bf16)
    rest = value - high.astype(f32)
    middle = rest.astype(bf16)
    low = (rest - middle.astype(f32)).astype(bf16)
    return high, middle, low


def iota(shape, dim):
    return lax.broadcasted_iota(jnp.int32, shape, dim)


def row_of(scalars, count):
    lane = iota((1, 128), 1)
    row = jnp.zeros((1, 128), f32)
    for c in range(count):
        row = jnp.where(lane == c, scalars[c], row)
    return row[:, 0:count]


def kernel(
    space, taps_hbm, cover_hbm, final_hbm, gain_hbm, sharp_hbm, lift_hbm, weights_hbm,
    channel_hbm, back_hbm, images_hbm, cleaned_hbm, lagrange_hbm, update_out, fine_out,
    cover, final_in, gain_in, sharp_in, tap_rows, lift_in, weights_in, taps_in,
    back_in, images, cleaned, lagrange, field, wide, part, parts_in, rows_pad,
    y_forward, y_adjoint, z_rows, xz_forward, xz_adjoint, spreads, lift, lift_final, weights, channel_taps,
    stack, deviations, normed, bands, conv, mixed, stats, gathered,
    local, send1, recv1, send2, recv2, send3, recv3, ready,
):
    group = lax.axis_index("groups")
    s = lax.axis_index("space")
    w = lax.axis_index("views")
    me = 2 * s + w
    count = 2 * space

    loads = [
        pltpu.make_async_copy(cleaned_hbm, cleaned, local.at[0]),
        pltpu.make_async_copy(lagrange_hbm, lagrange, local.at[1]),
        pltpu.make_async_copy(taps_hbm, tap_rows, local.at[3]),
        pltpu.make_async_copy(images_hbm, images, local.at[4]),
        pltpu.make_async_copy(cover_hbm, cover, local.at[5]),
        pltpu.make_async_copy(final_hbm, final_in, local.at[6]),
        pltpu.make_async_copy(gain_hbm, gain_in, local.at[7]),
        pltpu.make_async_copy(sharp_hbm, sharp_in, local.at[8]),
        pltpu.make_async_copy(lift_hbm, lift_in, local.at[9]),
        pltpu.make_async_copy(weights_hbm, weights_in, local.at[10]),
        pltpu.make_async_copy(channel_hbm, taps_in, local.at[11]),
        pltpu.make_async_copy(back_hbm, back_in, local.at[12]),
    ]
    for load in loads:
        load.start()

    def present(ds):
        if ds < 0:
            return s > 0
        if ds > 0:
            return s < space - 1
        return s >= 0

    def other(flip):
        return 1 - w if flip else w

    def peer(step):
        return lax.rem(me + step, count)

    barrier = pltpu.get_barrier_semaphore()

    for ds, flip in RELATIONS:

        @pl.when(present(ds))
        def _():
            pl.semaphore_signal(
                barrier, inc=1, device_id=(group, s + ds, other(flip)), device_id_type=MESH
            )

    loads[0].wait()
    loads[1].wait()
    field[...] = cleaned[...] - lagrange[...]
    wide[pl.ds(16 + 8 * w, 8)] = field[...]
    wide[0:6] = jnp.zeros((6,) + wide.shape[1:], f32)
    wide[42:48] = jnp.zeros((6,) + wide.shape[1:], f32)

    @pl.when(s == 0)
    def _():
        wide[6:16] = jnp.zeros((10,) + wide.shape[1:], f32)

    @pl.when(s == space - 1)
    def _():
        wide[32:42] = jnp.zeros((10,) + wide.shape[1:], f32)

    beside = 1 + 2 * present(-1).astype(jnp.int32) + 2 * present(1).astype(jnp.int32)
    pl.semaphore_wait(barrier, beside)

    spans = []
    while 2 << len(spans) < space - 1:
        spans.append(2 << len(spans))

    def tell(k):
        for side, at in enumerate((s - spans[k], s + spans[k])):

            @pl.when((at >= 0) & (at < space))
            def _():
                pl.semaphore_signal(
                    ready.at[k, 1 - side], inc=1, device_id=(group, at, w), device_id_type=MESH
                )

    def hear(k):
        for side, at in enumerate((s - spans[k], s + spans[k])):

            @pl.when((at >= 0) & (at < space))
            def _():
                pl.semaphore_wait(ready.at[k, side], 1)


    def first(k, ds, flip, sender_w):
        begin, size = 0, 8
        if (ds, sender_w) == (1, 0):
            begin, size = 6, 2
        if (ds, sender_w) == (-1, 1):
            begin, size = 0, 2
        return pltpu.make_async_remote_copy(
            src_ref=field.at[pl.ds(begin, size)],
            dst_ref=wide.at[pl.ds(16 * (1 - ds) + 8 * sender_w + begin, size)],
            send_sem=send1.at[k],
            recv_sem=recv1.at[k],
            device_id=(group, s + ds, other(flip)),
            device_id_type=MESH,
        )

    for k, (ds, flip) in enumerate(RELATIONS):
        for core in range(2):

            @pl.when(present(ds) & (w == core))
            def _():
                first(k, ds, flip, core).start()

    for load in loads[2:]:
        load.wait()
    rows = iota((128, 128), 0)
    cols = iota((128, 128), 1)
    keep_y = jnp.abs(rows - cols) <= 10
    lane_tile = iota((8, 128), 1) // 16
    rows_pad[...] = jnp.zeros_like(rows_pad)
    rows_pad[:, :, :, 0:21] = tap_rows[...]

    def build_y(v, carry):
        for r in range(2):
            row = pltpu.roll(rows_pad[v, 1], 118, 1)[r : r + 1]
            spread = pltpu.roll(
                jnp.broadcast_to(row, (128, 128)), 0, 1, stride=1, stride_axis=0
            )
            high, low = halves(jnp.where(keep_y, spread, 0.0))
            for k, value in enumerate((high, high, low)):
                y_forward[v, :, 384 * r + 128 * k : 384 * r + 128 * k + 128] = value
                y_adjoint[v, 128 * k : 128 * k + 128, 128 * r : 128 * r + 128] = value
        return carry

    lax.fori_loop(0, images.shape[0], build_y, 0, unroll=True)

    taps_x = jnp.concatenate([rows_pad[v, 0] for v in range(4)], axis=0)
    taps_z = jnp.concatenate([rows_pad[v, 2] for v in range(4)], axis=0)
    spot_x = iota((32, 896), 1)
    spot_z = iota((32, 1024), 1)
    distance = lax.rem(spot_z, 8) - spot_z // 128

    def picked(tap_values, wanted):
        rows_in = jnp.concatenate([piece[:, 0:32] for piece in thirds(tap_values)], axis=0)
        select = jnp.where(iota(wanted.shape, 0) == wanted, 1.0, 0.0).astype(bf16)
        found = jnp.dot(rows_in, select, preferred_element_type=f32)
        return found[0:8] + found[8:16] + found[16:24]

    bases_x = picked(
        taps_x, jnp.where(spot_x < 384, spot_x // 8 - 6, 35 - (spot_x - 384) // 8)
    )
    for mirrored in range(2):
        found = picked(taps_z, 10 - distance if mirrored else 10 + distance)
        for z in range(8):
            z_rows[8 * mirrored + z] = found[:, 128 * z : 128 * z + 128]

    for vr in range(8):
        pattern = z_rows[0:8, vr, :]
        base = jnp.concatenate([pattern] * 3, axis=1) * bases_x[vr : vr + 1, 0:384]
        for x in range(0, 16, 2):
            pair = [pltpu.roll(base, 8 * x, 1) if x else base, pltpu.roll(base, 8 * x + 8, 1)]
            high, low = halves(jnp.concatenate(pair, axis=0))
            at = 128 * vr + 8 * x
            xz_forward[at : at + 16, 0:384] = high
            xz_forward[at : at + 16, 384:768] = low
        pattern = z_rows[8:16, vr, :]
        base = jnp.concatenate([pattern] * 4, axis=1) * bases_x[vr : vr + 1, 384:896]
        for p in range(0, 36, 2):
            pair = []
            for q in (p, p + 1):
                begin = 8 * (35 - q)
                pair.append(base[:, begin : begin + 128])
            high, low = halves(jnp.concatenate(pair, axis=0))
            xz_adjoint[0, 8 * p : 8 * p + 16, 128 * vr : 128 * vr + 128] = high
            xz_adjoint[1, 8 * p : 8 * p + 16, 128 * vr : 128 * vr + 128] = low

    for k, (ds, flip) in enumerate(RELATIONS):
        for core in range(2):

            @pl.when(present(ds) & (w == core))
            def _():
                first(k, ds, flip, core).wait_send()

            @pl.when(present(-ds) & (other(flip) == core))
            def _():
                first(k, ds, flip, core).wait_recv()

    high, low = halves(wide[...].reshape(384, 128))
    field_stack = jnp.concatenate([high, low, high], axis=0)
    for v in range(4):
        along_xz = xz_forward[256 * v : 256 * v + 256, :]
        along_xz = jnp.concatenate([along_xz[:, 0:384], along_xz], axis=1)
        moved = jnp.dot(along_xz, field_stack, preferred_element_type=f32)
        pieces = []
        for r in range(2):
            high, low = halves(moved[128 * r : 128 * r + 128])
            pieces += [high, low, high]
        evolved = lax.dot_general(
            jnp.concatenate(pieces, axis=1), y_forward[v], NT, preferred_element_type=f32
        )
        mask = jnp.zeros((8, 128), f32)
        for j in range(8):
            mask = jnp.where(lane_tile == j, cover[v, 0, j].astype(f32), mask)
        residual = (evolved.reshape(16, 8, 128) - images[v].astype(f32)) * mask[None]
        high, low = halves(residual.reshape(128, 128))
        spread = jnp.dot(
            jnp.concatenate([high, low, high], axis=1), y_adjoint[v], preferred_element_type=f32
        )
        for r in range(2):
            high, low = halves(spread[:, 128 * r : 128 * r + 128])
            at = 256 * v + 128 * r
            spreads[at : at + 128, 0:128] = high
            spreads[at : at + 128, 128:256] = low

    def gather_rows(begin):
        at = slice(8 * begin, 8 * begin + 96)
        both = jnp.dot(xz_adjoint[0, at], spreads[...], preferred_element_type=f32)
        both = both[:, 0:128] + both[:, 128:256]
        both = both + jnp.dot(xz_adjoint[1, at], spreads[:, 0:128], preferred_element_type=f32)
        part[8 + begin : 20 + begin] = both.reshape(12, 8, 128)

    def second(k, ds, flip, target):
        begin, size = 0, 12
        if (ds, target) == (-1, 0):
            begin, size = 8, 4
        if (ds, target) == (1, 1):
            begin, size = 0, 4
        return pltpu.make_async_remote_copy(
            src_ref=part.at[pl.ds(8 * target + 16 + 16 * ds + begin, size)],
            dst_ref=parts_in.at[k, pl.ds(begin, size)],
            send_sem=send2.at[k],
            recv_sem=recv2.at[k],
            device_id=(group, s + ds, target),
            device_id_type=MESH,
        )

    for k, (ds, flip) in enumerate(RELATIONS):
        if k % 2 == 0:
            gather_rows((0, 24, 12)[k // 2])
        for core in range(2):

            @pl.when(present(ds) & (other(flip) == core))
            def _():
                second(k, ds, flip, core).start()

    for k, (ds, flip) in enumerate(RELATIONS):
        @pl.when(jnp.logical_not(present(-ds)))
        def _():
            parts_in[k] = jnp.zeros(parts_in.shape[1:], f32)

        if ds == -1:

            @pl.when(present(1) & (w == 0))
            def _():
                parts_in[k, 0:8] = jnp.zeros((8,) + parts_in.shape[2:], f32)

        if ds == 1:

            @pl.when(present(-1) & (w == 1))
            def _():
                parts_in[k, 4:12] = jnp.zeros((8,) + parts_in.shape[2:], f32)

    final_row = row_of(final_in, 48)
    gain_row = row_of(gain_in, 48)
    row48 = iota((48, 48), 0)
    col48 = iota((48, 48), 1)
    gain = jnp.sum(jnp.where(row48 == col48, gain_row, 0.0), axis=1, keepdims=True)
    gain_wide = jnp.broadcast_to(gain, (48, 1280))
    kernel_t = lift_in[...]
    centred = thirds(kernel_t - jnp.sum(kernel_t, axis=1, keepdims=True) * (1.0 / 48.0))
    mapped = thirds(
        jnp.broadcast_to(jnp.sum(kernel_t * final_row, axis=1, keepdims=True), (27, 16))
    )
    pieces = []
    for main, side in zip(centred, mapped):
        pieces.append(jnp.concatenate([main.astype(f32), side.astype(f32)], axis=1))
        pieces.append(jnp.zeros((5, 64), f32))
    stacked = jnp.concatenate(pieces, axis=0).astype(bf16)
    eye96 = jnp.where(iota((96, 96), 0) == iota((96, 96), 1), 1.0, 0.0).astype(bf16)
    lift_rows = lax.dot_general(stacked, eye96, TN, preferred_element_type=f32).astype(bf16)
    spot = iota((96, 512), 1)
    segment = spot // 80
    inner = lax.rem(spot, 80)
    piece_of = jnp.where(
        (segment <= 1) | (segment == 4), 0, jnp.where(segment == 5, 2, 1)
    )
    table_tap = lax.rem(iota((96, 512), 0), 32)
    fits = (iota((96, 512), 0) // 32 == piece_of) & (inner < 72) & (spot < 480)
    fits = fits & (table_tap < 27) & (table_tap // 9 == lax.rem(inner, 24) // 8)
    fits = fits & (lax.rem(table_tap, 3) == inner // 24)
    plane_of = jnp.where(fits, lax.rem(inner, 8) - lax.rem(table_tap, 9) // 3 + 1, 99)
    row16 = iota((16, 512), 0)
    final_sum = jnp.zeros((16, 512), f32)
    for z in range(8):
        table = jnp.where(plane_of == z, 1.0, 0.0).astype(bf16)
        found = jnp.dot(lift_rows, table, preferred_element_type=f32)
        lift[z] = found[0:48].astype(bf16)
        final_sum = jnp.where(row16 == z, found[48:64], final_sum)
    lift_final[...] = final_sum.astype(bf16)

    eye48 = jnp.where(row48 == col48, 1.0, 0.0)
    weights[...] = lax.dot_general(
        weights_in[...], eye48.astype(bf16), TN, preferred_element_type=f32
    ).astype(bf16)
    eye27 = jnp.where(iota((27, 128), 0) == iota((27, 128), 1), 1.0, 0.0)
    channel_taps[...] = lax.dot_general(
        taps_in[...], eye27, TN, precision=highest, preferred_element_type=f32
    )
    back = jnp.dot(
        final_row, back_in[...].astype(f32), precision=highest, preferred_element_type=f32
    )

    split_taps = jnp.concatenate(halves(channel_taps[...][:, 0:32]), axis=0)
    spot_c = iota((32, 768), 1)
    inner_c = lax.rem(spot_c, 256)
    conv_tap = iota((32, 768), 0)
    fits = (conv_tap < 27) & (conv_tap // 9 == inner_c // 64)
    fits = fits & (lax.rem(conv_tap, 3) == spot_c // 256)
    plane_of = jnp.where(fits, lax.rem(spot_c, 64) // 8 - lax.rem(conv_tap, 9) // 3 + 1, 99)
    own = lax.rem(iota((8, 192), 1), 8) == iota((8, 192), 0)
    for zz in range(4):
        tiles = []
        for half in range(2):
            table = jnp.where(plane_of == 2 * zz + half, 1.0, 0.0).astype(bf16)
            tiles.append(jnp.dot(split_taps, table, preferred_element_type=f32))
        for dy in range(3):
            lanes = slice(256 * dy, 256 * dy + 192)
            for g in range(18):
                for part_of in range(2):
                    row = 144 * part_of + 8 * g
                    pair = [jnp.where(own, tile[row : row + 8, lanes], 0.0) for tile in tiles]
                    block_rows = jnp.concatenate(pair, axis=0).astype(bf16)
                    conv[g, 64 * dy + 16 * zz : 64 * dy + 16 * zz + 16, 192 * part_of : 192 * part_of + 192] = (
                        block_rows
                    )

    for k, (ds, flip) in enumerate(RELATIONS):
        for core in range(2):

            @pl.when(present(ds) & (other(flip) == core))
            def _():
                second(k, ds, flip, core).wait_send()

            @pl.when(present(-ds) & (w == core))
            def _():
                second(k, ds, flip, core).wait_recv()

    if spans:
        tell(0)

    gradient = part[pl.ds(8 * w + 16, 12)]
    for k in range(5):
        gradient = gradient + parts_in[k]
    fine = wide[pl.ds(14 + 8 * w, 12)] - step_size * gradient
    row_id = 16 * s + 8 * w - 2 + iota(fine.shape, 0)
    fine = jnp.where((row_id >= 0) & (row_id < 16 * space), fine, 0.0)
    fine_out[...] = fine[2:10]

    lane3 = iota(fine.shape, 2)
    before = jnp.where(lane3 == 0, 0.0, pltpu.roll(fine, 1, 2))
    after = jnp.where(lane3 == 127, 0.0, pltpu.roll(fine, 127, 2))
    for x in range(10):
        pieces = []
        for moved in (before, fine, after):
            pieces.append(moved[x : x + 3].reshape(24, 128))
        pieces.append(jnp.zeros((8, 128), f32))
        high, middle, low = thirds(jnp.concatenate(pieces, axis=0))
        at = slice(x * 128, (x + 1) * 128)
        for k, piece in enumerate((high, middle, high, middle, low, high)):
            stack[80 * k : 80 * k + 80, at] = piece
    stack[480:512] = jnp.zeros((32, 1280), bf16)

    wide_row = 16 * s + 8 * w - 1 + iota((48, 1280), 1) // 128
    inside = (wide_row >= 0) & (wide_row < 16 * space)

    deviations[...] = jnp.dot(
        lift[...].reshape(384, 512), stack[...], preferred_element_type=f32
    ).reshape(8, 48, 1280)

    first_lane = iota((64, 128), 1) == 0
    last_lane = iota((64, 128), 1) == 127

    def spread_rows(zz, pair, first_group):
        rows = pl.ds(pl.multiple_of(16 * zz, 16), 16)
        for g in range(pair[0].shape[0] // 8):
            for x in range(10):
                at = slice(x * 128, (x + 1) * 128)
                cell = jnp.concatenate([proj[8 * g : 8 * g + 8, at] for proj in pair], axis=0)
                bands[first_group + g, rows, at] = cell.astype(bf16)

    def plane_pair(zz, carry):
        pair = []
        for half in range(2):
            dev = deviations[2 * zz + half]
            spread = jnp.sum(dev * dev, axis=0, keepdims=True) * (1.0 / 48.0)
            value = jnp.where(inside, dev * lax.rsqrt(spread + 1e-05) * gain_wide, 0.0)
            value = value.astype(bf16)
            normed[2 * zz + half] = value
            pair.append(jnp.dot(weights[0:96], value, preferred_element_type=f32))
        spread_rows(zz, pair, 0)
        return carry

    lax.fori_loop(0, 4, plane_pair, 0, unroll=4)

    def value_pair(zz, carry):
        pair = []
        for half in range(2):
            pair.append(
                jnp.dot(weights[96:144], normed[2 * zz + half], preferred_element_type=f32)
            )
        spread_rows(zz, pair, 12)
        return carry

    if spans:
        hear(0)
    if len(spans) > 1:
        tell(1)

    def channel_group(g, carry):
        at = pl.multiple_of(g * 8, 8)
        for n in range(4):
            pieces = []
            for dx in range(3):
                begin = dx * 128 + n * 256
                pieces.append(bands[g, :, begin : begin + 256])
            found = jnp.dot(
                conv[g], jnp.concatenate(pieces + pieces, axis=0), preferred_element_type=f32
            )
            found = [found[64 * dy : 64 * dy + 64] for dy in range(3)]
            for x in range(2):
                before, here, after = [part_of[:, 128 * x : 128 * x + 128] for part_of in found]
                total = here + jnp.where(first_lane, 0.0, pltpu.roll(before, 1, 1))
                total = total + jnp.where(last_lane, 0.0, pltpu.roll(after, 127, 1))
                columns = slice(n * 256 + x * 128, n * 256 + x * 128 + 128)
                for z in range(8):
                    mixed[z, pl.ds(at, 8), columns] = total[8 * z : 8 * z + 8]
        return carry

    lax.fori_loop(0, 12, channel_group, 0, unroll=6)

    def gram_step(z, total):
        value = mixed[z, 0:96].astype(bf16)
        return total + lax.dot_general(value, value, NT, preferred_element_type=f32)

    gram = lax.fori_loop(0, 8, gram_step, jnp.zeros((96, 96), f32), unroll=True)

    same = row48 // 12 == col48 // 12
    block = jnp.where(same, 1.0, 0.0)
    row16 = iota((16, 48), 0)
    col16 = iota((16, 48), 1)
    pick = jnp.where(lax.rem(col16, 12) == row16, 1.0, 0.0)
    kq = jnp.where(same, gram[48:96, 0:48], 0.0)
    squares_q = jnp.sum(jnp.where(row48 == col48, gram[0:48, 0:48], 0.0), axis=0, keepdims=True)
    squares_k = jnp.sum(jnp.where(row48 == col48, gram[48:96, 48:96], 0.0), axis=0, keepdims=True)
    packed = jnp.dot(pick, kq, precision=highest, preferred_element_type=f32)
    packed = jnp.where(row16 == 12, squares_q, packed)
    packed = jnp.where(row16 == 13, squares_k, packed)
    stats[...] = jnp.zeros_like(stats)
    stats[:, 0:48] = packed[0:8]
    stats[:, 64:112] = packed[8:16]

    for k in range(1, len(spans)):
        if k > 1:
            tell(k)
        hear(k)

    def share(step):
        to = peer(step)
        return pltpu.make_async_remote_copy(
            src_ref=stats,
            dst_ref=gathered.at[step],
            send_sem=send3.at[step],
            recv_sem=recv3.at[step],
            device_id=(group, to // 2, lax.rem(to, 2)),
            device_id_type=MESH,
        )

    def start(step, carry):
        share(step).start()
        return carry

    def finish(step, carry):
        share(step).wait()
        return carry

    lax.fori_loop(1, count, start, 0)
    gathered[0] = stats[...]
    lax.fori_loop(0, 4, value_pair, 0, unroll=4)
    lax.fori_loop(12, 18, channel_group, 0, unroll=6)
    update = jnp.dot(lift_final[...], stack[...], preferred_element_type=f32)
    lax.fori_loop(1, count, finish, 0)

    def add(step, total):
        slot = lax.rem(me - step + count, count)
        return total + gathered[slot]

    paired = lax.fori_loop(0, count, add, jnp.zeros((8, 128), f32))
    summed = jnp.concatenate([paired[:, 0:48], paired[:, 64:112]], axis=0)
    squares_q = summed[12:13]
    squares_k = summed[13:14]
    lengths_k = jnp.dot(
        pick * jnp.sqrt(squares_k + 1e-06), block, precision=highest, preferred_element_type=f32
    )
    valid = row16 < 12
    head = iota((1, 48), 1) // 12
    sharp_row = jnp.zeros((1, 48), f32)
    for h in range(4):
        sharp_row = jnp.where(head == h, sharp_in[h], sharp_row)
    logits = sharp_row * summed / (jnp.sqrt(squares_q + 1e-06) * jnp.where(valid, lengths_k, 1.0))
    raised = jnp.where(valid, jnp.exp(jnp.where(valid, logits, 0.0)), 0.0)
    shares = (raised / jnp.sum(raised, axis=0, keepdims=True)).astype(bf16).astype(f32)
    placed_shares = lax.dot_general(
        shares, pick, TN, precision=highest, preferred_element_type=f32
    )
    placed_shares = jnp.where(same, placed_shares, 0.0).astype(bf16)
    back_high, back_low = halves(back)

    def value_plane(z, total):
        attended = jnp.dot(
            placed_shares, mixed[z, 96:144].astype(bf16), preferred_element_type=f32
        )
        back_rows = jnp.where(row16 == z, back_high.astype(f32), 0.0)
        back_rows = jnp.where(row16 == z + 8, back_low.astype(f32), back_rows)
        return total + jnp.dot(
            back_rows.astype(bf16), attended.astype(bf16), preferred_element_type=f32
        )

    added = lax.fori_loop(0, 8, value_plane, jnp.zeros((16, 1024), f32), unroll=True)
    extra = added[0:8] + added[8:16]
    for x in range(8):
        update_out[x] = (
            update[0:8, (x + 1) * 128 : (x + 2) * 128] + extra[:, x * 128 : (x + 1) * 128]
        )


def body(
    space,
    acquired_images,
    blur_profile_coefficients,
    specimen_coverage,
    cleaned_estimate,
    lagrange_multiplier,
    lifting_kernel,
    standardize_factor,
    triple_lifting_kernel,
    per_channel_kernel,
    sharpness_factor,
    mixing_back_kernel,
    final_mapping_kernel,
):
    vmem = pl.BlockSpec(memory_space=pltpu.VMEM)
    hbm = pl.BlockSpec(memory_space=pltpu.HBM)
    profiles = blur_profile_coefficients.transpose(0, 2, 1, 3)
    count = 2 * space
    shape = pltpu.VMEM((8, 8, 128), f32)
    dma = pltpu.SemaphoreType.DMA
    update, fine = pl.pallas_call(
        functools.partial(kernel, space),
        out_shape=(shape, shape),
        in_specs=[hbm] * 12,
        out_specs=(vmem, vmem),
        scratch_shapes=[
            pltpu.SMEM((4, 1, 8), jnp.int32),
            pltpu.SMEM((48,), f32),
            pltpu.SMEM((48,), f32),
            pltpu.SMEM((4,), f32),
            pltpu.VMEM((4, 3, 2, 21), f32),
            pltpu.VMEM((27, 48), f32),
            pltpu.VMEM((48, 144), bf16),
            pltpu.VMEM((27, 144), f32),
            pltpu.VMEM((48, 48), bf16),
            pltpu.VMEM((4, 16, 8, 128), bf16),
            pltpu.VMEM((8, 8, 128), f32),
            pltpu.VMEM((8, 8, 128), f32),
            pltpu.VMEM((8, 8, 128), f32),
            pltpu.VMEM((48, 8, 128), f32),
            pltpu.VMEM((52, 8, 128), f32),
            pltpu.VMEM((5, 12, 8, 128), f32),
            pltpu.VMEM((4, 3, 2, 128), f32),
            pltpu.VMEM((4, 128, 768), bf16),
            pltpu.VMEM((4, 384, 256), bf16),
            pltpu.VMEM((16, 8, 128), f32),
            pltpu.VMEM((1024, 768), bf16),
            pltpu.VMEM((2, 288, 1024), bf16),
            pltpu.VMEM((1024, 256), bf16),
            pltpu.VMEM((8, 48, 512), bf16),
            pltpu.VMEM((16, 512), bf16),
            pltpu.VMEM((144, 48), bf16),
            pltpu.VMEM((144, 128), f32),
            pltpu.VMEM((512, 1280), bf16),
            pltpu.VMEM((8, 48, 1280), f32),
            pltpu.VMEM((8, 48, 1280), bf16),
            pltpu.VMEM((18, 64, 1280), bf16),
            pltpu.VMEM((18, 192, 384), bf16),
            pltpu.VMEM((8, 144, 1024), f32),
            pltpu.VMEM((8, 128), f32),
            pltpu.VMEM((count, 8, 128), f32),
            dma((13,)),
            dma((5,)),
            dma((5,)),
            dma((5,)),
            dma((5,)),
            dma((count,)),
            dma((count,)),
            pltpu.SemaphoreType.REGULAR((8, 2)),
        ],
        compiler_params=pltpu.CompilerParams(
            collective_id=0, has_side_effects=True, vmem_limit_bytes=66912256
        ),
        name="iteration",
    )(
        profiles,
        specimen_coverage,
        final_mapping_kernel,
        standardize_factor,
        sharpness_factor,
        lifting_kernel.T,
        triple_lifting_kernel.T,
        per_channel_kernel.T,
        mixing_back_kernel,
        acquired_images,
        cleaned_estimate,
        lagrange_multiplier,
    )
    new_denoised = fine + update
    new_dual = lagrange_multiplier + fine - new_denoised
    return new_denoised, new_dual


def solution(mesh):
    placed = (
        P("views", ("groups", "space"), None, None),
        P("views", None, None, None),
        P("views", ("groups", "space"), None),
        P(("groups", "space", "views"), None, None),
        P(("groups", "space", "views"), None, None),
        P(),
        P(),
        P(),
        P(),
        P(),
        P(),
        P(),
    )
    return jax.shard_map(
        functools.partial(body, mesh.shape["space"]),
        mesh=mesh,
        in_specs=placed,
        out_specs=(
            P(("groups", "space", "views"), None, None),
            P(("groups", "space", "views"), None, None),
        ),
        check_vma=False,
    )
```

```python
import functools

import jax
import jax.numpy as jnp
from jax import lax
from jax.experimental import pallas as pl
from jax.experimental.pallas import tpu as pltpu
from jax.sharding import PartitionSpec as P

highest = lax.Precision.HIGHEST
step_size = 0.5
MESH = pl.DeviceIdType.MESH
f32 = jnp.float32
bf16 = jnp.bfloat16
RELATIONS = ((-1, 0), (-1, 1), (1, 0), (1, 1), (0, 1))


def halves(value):
    high = value.astype(bf16)
    low = (value - high.astype(f32)).astype(bf16)
    return high, low


def dot3(left, right):
    lh, ll = left
    rh, rl = right
    return (
        jnp.dot(lh, rh, preferred_element_type=f32)
        + jnp.dot(lh, rl, preferred_element_type=f32)
        + jnp.dot(ll, rh, preferred_element_type=f32)
    )


NT = (((1,), (1,)), ((), ()))
TN = (((0,), (0,)), ((), ()))


def dotg3(left, right, dims):
    lh, ll = left
    rh, rl = right
    total = None
    for first, second in ((lh, rh), (lh, rl), (ll, rh)):
        term = lax.dot_general(first, second, dims, preferred_element_type=f32)
        total = term if total is None else total + term
    return total


def thirds(value):
    high = value.astype(bf16)
    rest = value - high.astype(f32)
    middle = rest.astype(bf16)
    low = (rest - middle.astype(f32)).astype(bf16)
    return high, middle, low


def iota(shape, dim):
    return lax.broadcasted_iota(jnp.int32, shape, dim)


def row_of(scalars, count):
    lane = iota((1, 128), 1)
    row = jnp.zeros((1, 128), f32)
    for c in range(count):
        row = jnp.where(lane == c, scalars[c], row)
    return row[:, 0:count]


def kernel(
    space, taps_hbm, cover_hbm, final_hbm, gain_hbm, sharp_hbm, lift_hbm, weights_hbm,
    channel_hbm, back_hbm, images_hbm, cleaned_hbm, lagrange_hbm, update_out, fine_out,
    cover, final_in, gain_in, sharp_in, tap_rows, lift_in, weights_in, taps_in,
    back_in, images, cleaned, lagrange, field, wide, part, parts_in, rows_pad,
    y_forward, y_adjoint, z_rows, xz_forward, xz_adjoint, spreads, lift, lift_final, weights, channel_taps,
    stack, deviations, normed, bands, conv, mixed, values, back_rows, stats, gathered,
    local, send1, recv1, send2, recv2, send3, recv3, ready,
):
    group = lax.axis_index("groups")
    s = lax.axis_index("space")
    w = lax.axis_index("views")
    me = 2 * s + w
    count = 2 * space

    loads = [
        pltpu.make_async_copy(cleaned_hbm, cleaned, local.at[0]),
        pltpu.make_async_copy(lagrange_hbm, lagrange, local.at[1]),
        pltpu.make_async_copy(taps_hbm, tap_rows, local.at[3]),
        pltpu.make_async_copy(images_hbm, images, local.at[4]),
        pltpu.make_async_copy(cover_hbm, cover, local.at[5]),
        pltpu.make_async_copy(final_hbm, final_in, local.at[6]),
        pltpu.make_async_copy(gain_hbm, gain_in, local.at[7]),
        pltpu.make_async_copy(sharp_hbm, sharp_in, local.at[8]),
        pltpu.make_async_copy(lift_hbm, lift_in, local.at[9]),
        pltpu.make_async_copy(weights_hbm, weights_in, local.at[10]),
        pltpu.make_async_copy(channel_hbm, taps_in, local.at[11]),
        pltpu.make_async_copy(back_hbm, back_in, local.at[12]),
    ]
    for load in loads:
        load.start()

    def present(ds):
        if ds < 0:
            return s > 0
        if ds > 0:
            return s < space - 1
        return s >= 0

    def other(flip):
        return 1 - w if flip else w

    def peer(step):
        return lax.rem(me + step, count)

    barrier = pltpu.get_barrier_semaphore()

    for ds, flip in RELATIONS:

        @pl.when(present(ds))
        def _():
            pl.semaphore_signal(
                barrier, inc=1, device_id=(group, s + ds, other(flip)), device_id_type=MESH
            )

    loads[0].wait()
    loads[1].wait()
    field[...] = cleaned[...] - lagrange[...]
    wide[pl.ds(16 + 8 * w, 8)] = field[...]
    wide[0:6] = jnp.zeros((6,) + wide.shape[1:], f32)
    wide[42:48] = jnp.zeros((6,) + wide.shape[1:], f32)

    @pl.when(s == 0)
    def _():
        wide[6:16] = jnp.zeros((10,) + wide.shape[1:], f32)

    @pl.when(s == space - 1)
    def _():
        wide[32:42] = jnp.zeros((10,) + wide.shape[1:], f32)

    beside = 1 + 2 * present(-1).astype(jnp.int32) + 2 * present(1).astype(jnp.int32)
    pl.semaphore_wait(barrier, beside)

    spans = []
    while 2 << len(spans) < space - 1:
        spans.append(2 << len(spans))

    def tell(k):
        for side, at in enumerate((s - spans[k], s + spans[k])):

            @pl.when((at >= 0) & (at < space))
            def _():
                pl.semaphore_signal(
                    ready.at[k, 1 - side], inc=1, device_id=(group, at, w), device_id_type=MESH
                )

    def hear(k):
        for side, at in enumerate((s - spans[k], s + spans[k])):

            @pl.when((at >= 0) & (at < space))
            def _():
                pl.semaphore_wait(ready.at[k, side], 1)


    def first(k, ds, flip, sender_w):
        begin, size = 0, 8
        if (ds, sender_w) == (1, 0):
            begin, size = 6, 2
        if (ds, sender_w) == (-1, 1):
            begin, size = 0, 2
        return pltpu.make_async_remote_copy(
            src_ref=field.at[pl.ds(begin, size)],
            dst_ref=wide.at[pl.ds(16 * (1 - ds) + 8 * sender_w + begin, size)],
            send_sem=send1.at[k],
            recv_sem=recv1.at[k],
            device_id=(group, s + ds, other(flip)),
            device_id_type=MESH,
        )

    for k, (ds, flip) in enumerate(RELATIONS):
        for core in range(2):

            @pl.when(present(ds) & (w == core))
            def _():
                first(k, ds, flip, core).start()

    for load in loads[2:]:
        load.wait()
    rows = iota((128, 128), 0)
    cols = iota((128, 128), 1)
    keep_y = jnp.abs(rows - cols) <= 10
    lane_tile = iota((8, 128), 1) // 16
    rows_pad[...] = jnp.zeros_like(rows_pad)
    rows_pad[:, :, :, 0:21] = tap_rows[...]

    def build_y(v, carry):
        for r in range(2):
            row = pltpu.roll(rows_pad[v, 1], 118, 1)[r : r + 1]
            spread = pltpu.roll(
                jnp.broadcast_to(row, (128, 128)), 0, 1, stride=1, stride_axis=0
            )
            high, low = halves(jnp.where(keep_y, spread, 0.0))
            for k, value in enumerate((high, high, low)):
                y_forward[v, :, 384 * r + 128 * k : 384 * r + 128 * k + 128] = value
                y_adjoint[v, 128 * k : 128 * k + 128, 128 * r : 128 * r + 128] = value
        return carry

    lax.fori_loop(0, images.shape[0], build_y, 0, unroll=True)

    taps_x = jnp.concatenate([rows_pad[v, 0] for v in range(4)], axis=0)
    taps_z = jnp.concatenate([rows_pad[v, 2] for v in range(4)], axis=0)
    spot_x = iota((32, 896), 1)
    spot_z = iota((32, 1024), 1)
    distance = lax.rem(spot_z, 8) - spot_z // 128

    def picked(tap_values, wanted):
        rows_in = jnp.concatenate([piece[:, 0:32] for piece in thirds(tap_values)], axis=0)
        select = jnp.where(iota(wanted.shape, 0) == wanted, 1.0, 0.0).astype(bf16)
        found = jnp.dot(rows_in, select, preferred_element_type=f32)
        return found[0:8] + found[8:16] + found[16:24]

    bases_x = picked(
        taps_x, jnp.where(spot_x < 384, spot_x // 8 - 6, 35 - (spot_x - 384) // 8)
    )
    for mirrored in range(2):
        found = picked(taps_z, 10 - distance if mirrored else 10 + distance)
        for z in range(8):
            z_rows[8 * mirrored + z] = found[:, 128 * z : 128 * z + 128]

    for vr in range(8):
        pattern = z_rows[0:8, vr, :]
        base = jnp.concatenate([pattern] * 3, axis=1) * bases_x[vr : vr + 1, 0:384]
        for x in range(0, 16, 2):
            pair = [pltpu.roll(base, 8 * x, 1) if x else base, pltpu.roll(base, 8 * x + 8, 1)]
            high, low = halves(jnp.concatenate(pair, axis=0))
            at = 128 * vr + 8 * x
            xz_forward[at : at + 16, 0:384] = high
            xz_forward[at : at + 16, 384:768] = low
        pattern = z_rows[8:16, vr, :]
        base = jnp.concatenate([pattern] * 4, axis=1) * bases_x[vr : vr + 1, 384:896]
        for p in range(0, 36, 2):
            pair = []
            for q in (p, p + 1):
                begin = 8 * (35 - q)
                pair.append(base[:, begin : begin + 128])
            high, low = halves(jnp.concatenate(pair, axis=0))
            xz_adjoint[0, 8 * p : 8 * p + 16, 128 * vr : 128 * vr + 128] = high
            xz_adjoint[1, 8 * p : 8 * p + 16, 128 * vr : 128 * vr + 128] = low

    for k, (ds, flip) in enumerate(RELATIONS):
        for core in range(2):

            @pl.when(present(ds) & (w == core))
            def _():
                first(k, ds, flip, core).wait_send()

            @pl.when(present(-ds) & (other(flip) == core))
            def _():
                first(k, ds, flip, core).wait_recv()

    high, low = halves(wide[...].reshape(384, 128))
    field_stack = jnp.concatenate([high, low, high], axis=0)
    for v in range(4):
        along_xz = xz_forward[256 * v : 256 * v + 256, :]
        along_xz = jnp.concatenate([along_xz[:, 0:384], along_xz], axis=1)
        moved = jnp.dot(along_xz, field_stack, preferred_element_type=f32)
        pieces = []
        for r in range(2):
            high, low = halves(moved[128 * r : 128 * r + 128])
            pieces += [high, low, high]
        evolved = lax.dot_general(
            jnp.concatenate(pieces, axis=1), y_forward[v], NT, preferred_element_type=f32
        )
        mask = jnp.zeros((8, 128), f32)
        for j in range(8):
            mask = jnp.where(lane_tile == j, cover[v, 0, j].astype(f32), mask)
        residual = (evolved.reshape(16, 8, 128) - images[v].astype(f32)) * mask[None]
        high, low = halves(residual.reshape(128, 128))
        spread = jnp.dot(
            jnp.concatenate([high, low, high], axis=1), y_adjoint[v], preferred_element_type=f32
        )
        for r in range(2):
            high, low = halves(spread[:, 128 * r : 128 * r + 128])
            at = 256 * v + 128 * r
            spreads[at : at + 128, 0:128] = high
            spreads[at : at + 128, 128:256] = low

    def gather_rows(begin):
        at = slice(8 * begin, 8 * begin + 96)
        both = jnp.dot(xz_adjoint[0, at], spreads[...], preferred_element_type=f32)
        both = both[:, 0:128] + both[:, 128:256]
        both = both + jnp.dot(xz_adjoint[1, at], spreads[:, 0:128], preferred_element_type=f32)
        part[8 + begin : 20 + begin] = both.reshape(12, 8, 128)

    def second(k, ds, flip, target):
        begin, size = 0, 12
        if (ds, target) == (-1, 0):
            begin, size = 8, 4
        if (ds, target) == (1, 1):
            begin, size = 0, 4
        return pltpu.make_async_remote_copy(
            src_ref=part.at[pl.ds(8 * target + 16 + 16 * ds + begin, size)],
            dst_ref=parts_in.at[k, pl.ds(begin, size)],
            send_sem=send2.at[k],
            recv_sem=recv2.at[k],
            device_id=(group, s + ds, target),
            device_id_type=MESH,
        )

    for k, (ds, flip) in enumerate(RELATIONS):
        if k % 2 == 0:
            gather_rows((0, 24, 12)[k // 2])
        for core in range(2):

            @pl.when(present(ds) & (other(flip) == core))
            def _():
                second(k, ds, flip, core).start()

    for k, (ds, flip) in enumerate(RELATIONS):
        @pl.when(jnp.logical_not(present(-ds)))
        def _():
            parts_in[k] = jnp.zeros(parts_in.shape[1:], f32)

        if ds == -1:

            @pl.when(present(1) & (w == 0))
            def _():
                parts_in[k, 0:8] = jnp.zeros((8,) + parts_in.shape[2:], f32)

        if ds == 1:

            @pl.when(present(-1) & (w == 1))
            def _():
                parts_in[k, 4:12] = jnp.zeros((8,) + parts_in.shape[2:], f32)

    final_row = row_of(final_in, 48)
    gain_row = row_of(gain_in, 48)
    row48 = iota((48, 48), 0)
    col48 = iota((48, 48), 1)
    gain = jnp.sum(jnp.where(row48 == col48, gain_row, 0.0), axis=1, keepdims=True)
    gain_wide = jnp.broadcast_to(gain, (48, 1280))
    kernel_t = lift_in[...]
    centred = thirds(kernel_t - jnp.sum(kernel_t, axis=1, keepdims=True) * (1.0 / 48.0))
    mapped = thirds(
        jnp.broadcast_to(jnp.sum(kernel_t * final_row, axis=1, keepdims=True), (27, 16))
    )
    pieces = []
    for main, side in zip(centred, mapped):
        pieces.append(jnp.concatenate([main.astype(f32), side.astype(f32)], axis=1))
        pieces.append(jnp.zeros((5, 64), f32))
    stacked = jnp.concatenate(pieces, axis=0).astype(bf16)
    eye96 = jnp.where(iota((96, 96), 0) == iota((96, 96), 1), 1.0, 0.0).astype(bf16)
    lift_rows = lax.dot_general(stacked, eye96, TN, preferred_element_type=f32).astype(bf16)
    spot = iota((96, 512), 1)
    segment = spot // 80
    inner = lax.rem(spot, 80)
    piece_of = jnp.where(
        (segment <= 1) | (segment == 4), 0, jnp.where(segment == 5, 2, 1)
    )
    table_tap = lax.rem(iota((96, 512), 0), 32)
    fits = (iota((96, 512), 0) // 32 == piece_of) & (inner < 72) & (spot < 480)
    fits = fits & (table_tap < 27) & (table_tap // 9 == lax.rem(inner, 24) // 8)
    fits = fits & (lax.rem(table_tap, 3) == inner // 24)
    plane_of = jnp.where(fits, lax.rem(inner, 8) - lax.rem(table_tap, 9) // 3 + 1, 99)
    row16 = iota((16, 512), 0)
    final_sum = jnp.zeros((16, 512), f32)
    for z in range(8):
        table = jnp.where(plane_of == z, 1.0, 0.0).astype(bf16)
        found = jnp.dot(lift_rows, table, preferred_element_type=f32)
        lift[z] = found[0:48].astype(bf16)
        final_sum = jnp.where(row16 == z, found[48:64], final_sum)
    lift_final[...] = final_sum.astype(bf16)

    eye48 = jnp.where(row48 == col48, 1.0, 0.0)
    weights[...] = lax.dot_general(
        weights_in[...], eye48.astype(bf16), TN, preferred_element_type=f32
    ).astype(bf16)
    eye27 = jnp.where(iota((27, 128), 0) == iota((27, 128), 1), 1.0, 0.0)
    channel_taps[...] = lax.dot_general(
        taps_in[...], eye27, TN, precision=highest, preferred_element_type=f32
    )
    back = jnp.dot(
        final_row, back_in[...].astype(f32), precision=highest, preferred_element_type=f32
    )
    channel_of = lax.rem(iota((48, 384), 1), 48) == iota((48, 384), 0)
    back_wide = jnp.dot(
        back, jnp.where(channel_of, 1.0, 0.0), precision=highest, preferred_element_type=f32
    )
    high, low = halves(back_wide)
    plane_row = iota((16, 384), 0)
    plane_lane = iota((16, 384), 1) // 48
    placed_back = jnp.where(plane_row == plane_lane, high.astype(f32), 0.0)
    placed_back = jnp.where(plane_row == plane_lane + 8, low.astype(f32), placed_back)
    back_rows[...] = placed_back.astype(bf16)

    split_taps = jnp.concatenate(halves(channel_taps[...][:, 0:32]), axis=0)
    spot_c = iota((32, 768), 1)
    inner_c = lax.rem(spot_c, 256)
    conv_tap = iota((32, 768), 0)
    fits = (conv_tap < 27) & (conv_tap // 9 == inner_c // 64)
    fits = fits & (lax.rem(conv_tap, 3) == spot_c // 256)
    plane_of = jnp.where(fits, lax.rem(spot_c, 64) // 8 - lax.rem(conv_tap, 9) // 3 + 1, 99)
    own = lax.rem(iota((8, 192), 1), 8) == iota((8, 192), 0)
    for zz in range(4):
        tiles = []
        for half in range(2):
            table = jnp.where(plane_of == 2 * zz + half, 1.0, 0.0).astype(bf16)
            tiles.append(jnp.dot(split_taps, table, preferred_element_type=f32))
        for dy in range(3):
            lanes = slice(256 * dy, 256 * dy + 192)
            for g in range(18):
                for part_of in range(2):
                    row = 144 * part_of + 8 * g
                    pair = [jnp.where(own, tile[row : row + 8, lanes], 0.0) for tile in tiles]
                    block_rows = jnp.concatenate(pair, axis=0).astype(bf16)
                    conv[g, 64 * dy + 16 * zz : 64 * dy + 16 * zz + 16, 192 * part_of : 192 * part_of + 192] = (
                        block_rows
                    )

    for k, (ds, flip) in enumerate(RELATIONS):
        for core in range(2):

            @pl.when(present(ds) & (other(flip) == core))
            def _():
                second(k, ds, flip, core).wait_send()

            @pl.when(present(-ds) & (w == core))
            def _():
                second(k, ds, flip, core).wait_recv()

    if spans:
        tell(0)

    gradient = part[pl.ds(8 * w + 16, 12)]
    for k in range(5):
        gradient = gradient + parts_in[k]
    fine = wide[pl.ds(14 + 8 * w, 12)] - step_size * gradient
    row_id = 16 * s + 8 * w - 2 + iota(fine.shape, 0)
    fine = jnp.where((row_id >= 0) & (row_id < 16 * space), fine, 0.0)
    fine_out[...] = fine[2:10]

    lane3 = iota(fine.shape, 2)
    before = jnp.where(lane3 == 0, 0.0, pltpu.roll(fine, 1, 2))
    after = jnp.where(lane3 == 127, 0.0, pltpu.roll(fine, 127, 2))
    for x in range(10):
        pieces = []
        for moved in (before, fine, after):
            pieces.append(moved[x : x + 3].reshape(24, 128))
        pieces.append(jnp.zeros((8, 128), f32))
        high, middle, low = thirds(jnp.concatenate(pieces, axis=0))
        at = slice(x * 128, (x + 1) * 128)
        for k, piece in enumerate((high, middle, high, middle, low, high)):
            stack[80 * k : 80 * k + 80, at] = piece
    stack[480:512] = jnp.zeros((32, 1280), bf16)

    wide_row = 16 * s + 8 * w - 1 + iota((48, 1280), 1) // 128
    inside = (wide_row >= 0) & (wide_row < 16 * space)

    deviations[...] = jnp.dot(
        lift[...].reshape(384, 512), stack[...], preferred_element_type=f32
    ).reshape(8, 48, 1280)

    first_lane = iota((64, 128), 1) == 0
    last_lane = iota((64, 128), 1) == 127

    def spread_rows(zz, pair, first_group):
        rows = pl.ds(pl.multiple_of(16 * zz, 16), 16)
        for g in range(pair[0].shape[0] // 8):
            for x in range(10):
                at = slice(x * 128, (x + 1) * 128)
                cell = jnp.concatenate([proj[8 * g : 8 * g + 8, at] for proj in pair], axis=0)
                bands[first_group + g, rows, at] = cell.astype(bf16)

    def plane_pair(zz, carry):
        pair = []
        for half in range(2):
            dev = deviations[2 * zz + half]
            spread = jnp.sum(dev * dev, axis=0, keepdims=True) * (1.0 / 48.0)
            value = jnp.where(inside, dev * lax.rsqrt(spread + 1e-05) * gain_wide, 0.0)
            value = value.astype(bf16)
            normed[2 * zz + half] = value
            pair.append(jnp.dot(weights[0:96], value, preferred_element_type=f32))
        spread_rows(zz, pair, 0)
        return carry

    lax.fori_loop(0, 4, plane_pair, 0, unroll=4)

    def value_pair(zz, carry):
        pair = []
        for half in range(2):
            pair.append(
                jnp.dot(weights[96:144], normed[2 * zz + half], preferred_element_type=f32)
            )
        spread_rows(zz, pair, 12)
        return carry

    if spans:
        hear(0)
    if len(spans) > 1:
        tell(1)

    def channel_group(g, carry):
        at = pl.multiple_of(g * 8, 8)
        for n in range(4):
            pieces = []
            for dx in range(3):
                begin = dx * 128 + n * 256
                pieces.append(bands[g, :, begin : begin + 256])
            found = jnp.dot(
                conv[g], jnp.concatenate(pieces + pieces, axis=0), preferred_element_type=f32
            )
            found = [found[64 * dy : 64 * dy + 64] for dy in range(3)]
            for x in range(2):
                before, here, after = [part_of[:, 128 * x : 128 * x + 128] for part_of in found]
                total = here + jnp.where(first_lane, 0.0, pltpu.roll(before, 1, 1))
                total = total + jnp.where(last_lane, 0.0, pltpu.roll(after, 127, 1))
                columns = slice(n * 256 + x * 128, n * 256 + x * 128 + 128)
                for z in range(8):
                    mixed[z, pl.ds(at, 8), columns] = total[8 * z : 8 * z + 8]
        return carry

    lax.fori_loop(0, 12, channel_group, 0, unroll=6)

    def gram_step(z, total):
        value = mixed[z, 0:96].astype(bf16)
        return total + lax.dot_general(value, value, NT, preferred_element_type=f32)

    gram = lax.fori_loop(0, 8, gram_step, jnp.zeros((96, 96), f32), unroll=True)

    same = row48 // 12 == col48 // 12
    block = jnp.where(same, 1.0, 0.0)
    row16 = iota((16, 48), 0)
    col16 = iota((16, 48), 1)
    pick = jnp.where(lax.rem(col16, 12) == row16, 1.0, 0.0)
    kq = jnp.where(same, gram[48:96, 0:48], 0.0)
    squares_q = jnp.sum(jnp.where(row48 == col48, gram[0:48, 0:48], 0.0), axis=0, keepdims=True)
    squares_k = jnp.sum(jnp.where(row48 == col48, gram[48:96, 48:96], 0.0), axis=0, keepdims=True)
    packed = jnp.dot(pick, kq, precision=highest, preferred_element_type=f32)
    packed = jnp.where(row16 == 12, squares_q, packed)
    packed = jnp.where(row16 == 13, squares_k, packed)
    stats[...] = jnp.zeros_like(stats)
    stats[:, 0:48] = packed[0:8]
    stats[:, 64:112] = packed[8:16]

    for k in range(1, len(spans)):
        if k > 1:
            tell(k)
        hear(k)

    def share(step):
        to = peer(step)
        return pltpu.make_async_remote_copy(
            src_ref=stats,
            dst_ref=gathered.at[step],
            send_sem=send3.at[step],
            recv_sem=recv3.at[step],
            device_id=(group, to // 2, lax.rem(to, 2)),
            device_id_type=MESH,
        )

    def start(step, carry):
        share(step).start()
        return carry

    def finish(step, carry):
        share(step).wait()
        return carry

    lax.fori_loop(1, count, start, 0)
    gathered[0] = stats[...]
    lax.fori_loop(0, 4, value_pair, 0, unroll=4)
    lax.fori_loop(12, 18, channel_group, 0, unroll=6)
    for z in range(8):
        values[z] = mixed[z, 96:144].astype(bf16)
    update = jnp.dot(lift_final[...], stack[...], preferred_element_type=f32)
    lax.fori_loop(1, count, finish, 0)

    def add(step, total):
        slot = lax.rem(me - step + count, count)
        return total + gathered[slot]

    paired = lax.fori_loop(0, count, add, jnp.zeros((8, 128), f32), unroll=16)
    summed = jnp.concatenate([paired[:, 0:48], paired[:, 64:112]], axis=0)
    squares_q = summed[12:13]
    squares_k = summed[13:14]
    lengths_k = jnp.dot(
        pick * jnp.sqrt(squares_k + 1e-06), block, precision=highest, preferred_element_type=f32
    )
    valid = row16 < 12
    head = iota((1, 48), 1) // 12
    sharp_row = jnp.zeros((1, 48), f32)
    for h in range(4):
        sharp_row = jnp.where(head == h, sharp_in[h], sharp_row)
    logits = sharp_row * summed / (jnp.sqrt(squares_q + 1e-06) * jnp.where(valid, lengths_k, 1.0))
    raised = jnp.where(valid, jnp.exp(jnp.where(valid, logits, 0.0)), 0.0)
    shares = (raised / jnp.sum(raised, axis=0, keepdims=True)).astype(bf16)
    placed_shares = lax.dot_general(
        shares, pick.astype(bf16), TN, preferred_element_type=f32
    )
    placed_shares = jnp.where(same, placed_shares, 0.0).astype(bf16)
    attended = [
        jnp.dot(placed_shares, values[z], preferred_element_type=f32).astype(bf16)
        for z in range(8)
    ]
    added = jnp.dot(
        back_rows[...], jnp.concatenate(attended, axis=0), preferred_element_type=f32
    )
    extra = added[0:8] + added[8:16]
    for x in range(8):
        update_out[x] = (
            update[0:8, (x + 1) * 128 : (x + 2) * 128] + extra[:, x * 128 : (x + 1) * 128]
        )


def body(
    space,
    acquired_images,
    blur_profile_coefficients,
    specimen_coverage,
    cleaned_estimate,
    lagrange_multiplier,
    lifting_kernel,
    standardize_factor,
    triple_lifting_kernel,
    per_channel_kernel,
    sharpness_factor,
    mixing_back_kernel,
    final_mapping_kernel,
):
    vmem = pl.BlockSpec(memory_space=pltpu.VMEM)
    hbm = pl.BlockSpec(memory_space=pltpu.HBM)
    profiles = blur_profile_coefficients.transpose(0, 2, 1, 3)
    count = 2 * space
    shape = pltpu.VMEM((8, 8, 128), f32)
    dma = pltpu.SemaphoreType.DMA
    update, fine = pl.pallas_call(
        functools.partial(kernel, space),
        out_shape=(shape, shape),
        in_specs=[hbm] * 12,
        out_specs=(vmem, vmem),
        scratch_shapes=[
            pltpu.SMEM((4, 1, 8), jnp.int32),
            pltpu.SMEM((48,), f32),
            pltpu.SMEM((48,), f32),
            pltpu.SMEM((4,), f32),
            pltpu.VMEM((4, 3, 2, 21), f32),
            pltpu.VMEM((27, 48), f32),
            pltpu.VMEM((48, 144), bf16),
            pltpu.VMEM((27, 144), f32),
            pltpu.VMEM((48, 48), bf16),
            pltpu.VMEM((4, 16, 8, 128), bf16),
            pltpu.VMEM((8, 8, 128), f32),
            pltpu.VMEM((8, 8, 128), f32),
            pltpu.VMEM((8, 8, 128), f32),
            pltpu.VMEM((48, 8, 128), f32),
            pltpu.VMEM((52, 8, 128), f32),
            pltpu.VMEM((5, 12, 8, 128), f32),
            pltpu.VMEM((4, 3, 2, 128), f32),
            pltpu.VMEM((4, 128, 768), bf16),
            pltpu.VMEM((4, 384, 256), bf16),
            pltpu.VMEM((16, 8, 128), f32),
            pltpu.VMEM((1024, 768), bf16),
            pltpu.VMEM((2, 288, 1024), bf16),
            pltpu.VMEM((1024, 256), bf16),
            pltpu.VMEM((8, 48, 512), bf16),
            pltpu.VMEM((16, 512), bf16),
            pltpu.VMEM((144, 48), bf16),
            pltpu.VMEM((144, 128), f32),
            pltpu.VMEM((512, 1280), bf16),
            pltpu.VMEM((8, 48, 1280), f32),
            pltpu.VMEM((8, 48, 1280), bf16),
            pltpu.VMEM((18, 64, 1280), bf16),
            pltpu.VMEM((18, 192, 384), bf16),
            pltpu.VMEM((8, 144, 1024), f32),
            pltpu.VMEM((8, 48, 1024), bf16),
            pltpu.VMEM((16, 384), bf16),
            pltpu.VMEM((8, 128), f32),
            pltpu.VMEM((count, 8, 128), f32),
            dma((13,)),
            dma((5,)),
            dma((5,)),
            dma((5,)),
            dma((5,)),
            dma((count,)),
            dma((count,)),
            pltpu.SemaphoreType.REGULAR((8, 2)),
        ],
        compiler_params=pltpu.CompilerParams(
            collective_id=0, has_side_effects=True, vmem_limit_bytes=66912256
        ),
        name="iteration",
    )(
        profiles,
        specimen_coverage,
        final_mapping_kernel,
        standardize_factor,
        sharpness_factor,
        lifting_kernel.T,
        triple_lifting_kernel.T,
        per_channel_kernel.T,
        mixing_back_kernel,
        acquired_images,
        cleaned_estimate,
        lagrange_multiplier,
    )
    new_denoised = fine + update
    new_dual = lagrange_multiplier + fine - new_denoised
    return new_denoised, new_dual


def solution(mesh):
    placed = (
        P("views", ("groups", "space"), None, None),
        P("views", None, None, None),
        P("views", ("groups", "space"), None),
        P(("groups", "space", "views"), None, None),
        P(("groups", "space", "views"), None, None),
        P(),
        P(),
        P(),
        P(),
        P(),
        P(),
        P(),
    )
    return jax.shard_map(
        functools.partial(body, mesh.shape["space"]),
        mesh=mesh,
        in_specs=placed,
        out_specs=(
            P(("groups", "space", "views"), None, None),
            P(("groups", "space", "views"), None, None),
        ),
        check_vma=False,
    )
```
